32 devices in a mesh: box: 8 (over z, y), col: 4 (over x, core).
Axes of the slice: x: 2, y: 2, z: 4, core: 2. Of those that a mesh axis runs over, the one named last changes fastest.
Arguments:
- box_points: float32 [16, 3, 512], P('box'), may hold values from 0 to 1
- proxy_directions: float32 [3, 1024], P(None, 'col'), may hold values from -1 to 1, as said below
- point_order: int32 [16, 512], P('box'), may hold values from 0 to 511, each once within a row
- neighbour_boxes: int32 [16, 8], P('box'), may hold values from 0 to 15, as said below
- neighbour_places: int32 [16, 8], P('box'), may hold values from 0 to 25
- pivot_inverse: float32 [16, 2, 256], P('box', None, 'col'), may hold values from -6 to 6
Outputs:
- interpolation: float32 [16, 2, 256, 256], P('box', None, None, 'col')
- skeleton_update: float32 [16, 2, 256, 256], P('box', None, 'col')
The draws below stay inside these ranges and needn't reach their ends.
Inputs may be any that keep to these rules, and one draw needn't show every extreme that they name: `neighbour_boxes`: box g is held by index g // 2 of the box axis. Every entry names a box of the same index or of the index just before or just after it, cyclically. Of the 16 entries of one index's boxes exactly half name boxes of that same index, never the listing box itself; a box may be listed twice in one row. `proxy_directions`: unit vectors.
All inputs are finite; a program needn't handle non-finite values.
Results may differ from the reference program's by a relative error of at most 0.0038.
Values sent between devices are 32-bit elements; how exact they have to be, the bound alone decides.
A program may use at most 64 MiB of HBM per device.

```python
import math
import jax
import jax.numpy as jnp
from jax import lax

P_SIZE = 512
S = 256
PROXY = 1024
NB = 8
BOX_DEV = 2
R = 256
BOXES = 16


def draw_proxy_directions(key, part):
    samples = jax.random.normal(key, (3, PROXY), jnp.float32)
    length = jnp.sqrt(jnp.sum(samples * samples, axis=0, keepdims=True)) + 1e-06
    return samples / length


def draw_neighbour_boxes(key, part):
    device_count = BOXES // BOX_DEV
    entries = BOX_DEV * NB
    key_list = jax.random.split(jax.random.fold_in(key, 17), 4)
    places = jax.vmap(lambda one_key: jax.random.permutation(one_key, entries))(jax.random.split(key_list[0], device_count))
    side_sign = 2 * jax.random.randint(key_list[1], (device_count, entries), 0, 2) - 1
    entry_rank = jnp.arange(entries, dtype=jnp.int32)[None, :]
    own_side = entry_rank < entries // 2
    device_step = jnp.where(own_side, 0, side_sign)
    home_box = places // NB
    own_slot = (home_box + 1 + jax.random.randint(key_list[2], (device_count, entries), 0, BOX_DEV - 1)) % BOX_DEV
    far_slot = jax.random.randint(key_list[3], (device_count, entries), 0, BOX_DEV)
    chosen_slot = jnp.where(own_side, own_slot, far_slot)
    device_rank = jnp.arange(device_count, dtype=jnp.int32)[:, None]
    target = (device_rank + device_step) % device_count * BOX_DEV + chosen_slot
    neighbour_table = jnp.zeros((device_count, entries), jnp.int32).at[device_rank, places].set(target.astype(jnp.int32))
    return neighbour_table.reshape(BOXES, NB)


def place_ends(values, rng, smallest, high):
    longest = values.shape.index(max(values.shape))
    spots = []
    for shift in (0, 1):
        where = [jax.random.randint(jax.random.fold_in(rng, axis), (), 0, length) for axis, length in enumerate(values.shape)]
        where[longest] = (where[longest] + shift) % values.shape[longest]
        spots.append(tuple(where))
    return values.at[spots[0]].set(smallest).at[spots[1]].set(high)


def steps_of(stream_key, dims, shards, least, high):
    level = 1.0
    for position, parts in shards:
        steps = jax.random.uniform(jax.random.fold_in(jax.random.fold_in(stream_key, 6), position), (parts,), jnp.float32, least / len(shards), high / len(shards))
        level = level * jnp.repeat(jnp.exp(steps), dims[position] // parts).reshape((-1,) + (1,) * (len(dims) - 1 - position))
    return level


def noise(rng, shape, scale, limit, pieces=(), kind=jnp.bfloat16):
    array = jax.random.normal(rng, shape, jnp.float32) * scale
    if len(pieces) > 0:
        array = steps_of(rng, shape, pieces, -0.22, 0.18) * array
    return jnp.clip(array, min=-limit, max=limit).astype(kind)


def setup_inputs(seed: int = 0) -> dict:
    key_of = jax.random.split(jax.random.key(seed), 7)
    box_points = jnp.clip(1.0 * jax.random.uniform(key_of[0], (BOXES, 3, P_SIZE), jnp.float32) ** steps_of(key_of[0], (BOXES, 3, P_SIZE), ((0, 8),), -0.2, 0.2), 0.0, 1.0)
    proxy_directions = draw_proxy_directions(jax.random.fold_in(key_of[6], 71), 0)
    point_order = jax.vmap(lambda own: jax.random.permutation(own, P_SIZE))(jax.random.split(key_of[2], BOXES)).reshape((BOXES, P_SIZE)).astype(jnp.int32)
    neighbour_boxes = draw_neighbour_boxes(jax.random.fold_in(key_of[6], 71), 0)
    neighbour_places = place_ends(jax.random.randint(key_of[4], (BOXES, NB), 0, 26), jax.random.fold_in(key_of[4], 1), 0, 25).astype(jnp.int32)
    pivot_inverse = noise(key_of[5], (BOXES, 2, R), 1.0, 6.0, ((0, 8), (2, 4)), jnp.float32)
    return {"box_points": box_points, "proxy_directions": proxy_directions, "point_order": point_order, "neighbour_boxes": neighbour_boxes, "neighbour_places": neighbour_places, "pivot_inverse": pivot_inverse}


wavenumber = 4.0 * math.pi
softening = 0.05
proxy_radius = 1.5
ridge_share = 0.05
highest = lax.Precision.HIGHEST

def helmholtz(targets, sources):
    distance_sq = jnp.zeros((targets.shape[1], sources.shape[1]), targets.dtype)
    for axis_id in range(3):
        difference = targets[axis_id][:, None] - sources[axis_id][None, :]
        distance_sq = distance_sq + difference * difference
    radius = jnp.sqrt(distance_sq + softening * softening)
    amplitude = 1.0 / (4.0 * math.pi * radius)
    return (amplitude * jnp.cos(wavenumber * radius), amplitude * jnp.sin(wavenumber * radius))

def decode(place_codes):
    full_code = place_codes + (place_codes >= 13).astype(jnp.int32)
    return jnp.stack([full_code // 9 - 1, full_code // 3 % 3 - 1, full_code % 3 - 1], axis=-1).astype(jnp.float32)

def cross_products(real_tile, imag_tile, skel_count):
    stacked = jnp.concatenate([real_tile, imag_tile], axis=0)
    flipped = jnp.concatenate([imag_tile, -real_tile], axis=0)
    left_cols = stacked[:, :skel_count]
    contract = (((0,), (0,)), ((), ()))
    real_cross = lax.dot_general(left_cols.astype(jnp.float32), stacked.astype(jnp.float32), contract, preferred_element_type=jnp.float32)
    imag_cross = lax.dot_general(left_cols.astype(jnp.float32), flipped.astype(jnp.float32), contract, preferred_element_type=jnp.float32)
    return jnp.stack([real_cross, imag_cross])

def factor(gram_block):
    real_gram = gram_block[0]
    imag_gram = gram_block[1]
    skel_count = real_gram.shape[0]
    ridge_value = ridge_share * jnp.trace(real_gram) / skel_count
    real_gram = real_gram + ridge_value * jnp.eye(skel_count, dtype=real_gram.dtype)
    upper_half = jnp.concatenate([real_gram, -imag_gram], axis=1)
    lower_half = jnp.concatenate([imag_gram, real_gram], axis=1)
    return jnp.linalg.cholesky(jnp.concatenate([upper_half, lower_half], axis=0))

def apply_inverse(cholesky_factor, right_side):
    stacked = right_side.reshape(2 * right_side.shape[1], right_side.shape[2])
    forward = lax.linalg.triangular_solve(cholesky_factor, stacked, left_side=True, lower=True)
    backward = lax.linalg.triangular_solve(cholesky_factor, forward, left_side=True, lower=True, transpose_a=True)
    return backward.reshape(right_side.shape)

def pair_update(near_points, own_columns, coefficients, pivot_row):
    skel_count = coefficients.shape[1]
    real_kernel, imag_kernel = helmholtz(near_points, own_columns)
    real_skel = real_kernel[:, :skel_count]
    imag_skel = imag_kernel[:, :skel_count]
    real_rest = real_kernel[:, skel_count:]
    imag_rest = imag_kernel[:, skel_count:]
    matmul_dims = (((1,), (0,)), ((), ()))
    outer_dims = (((1,), (1,)), ((), ()))

    def product(left_side, right_side):
        return lax.dot_general(left_side.astype(jnp.float32), right_side.astype(jnp.float32), matmul_dims, precision=highest, preferred_element_type=jnp.float32)

    def outer_product(left_side, right_side):
        return lax.dot_general(left_side.astype(jnp.float32), right_side.astype(jnp.float32), outer_dims, precision=highest, preferred_element_type=jnp.float32)
    real_block = real_rest - (product(real_skel, coefficients[0]) - product(imag_skel, coefficients[1]))
    imag_block = imag_rest - (product(real_skel, coefficients[1]) + product(imag_skel, coefficients[0]))
    real_weighted = real_block * pivot_row[0][None, :] - imag_block * pivot_row[1][None, :]
    imag_weighted = real_block * pivot_row[1][None, :] + imag_block * pivot_row[0][None, :]
    real_update = outer_product(real_weighted, real_block) - outer_product(imag_weighted, imag_block)
    imag_update = outer_product(real_weighted, imag_block) + outer_product(imag_weighted, real_block)
    return -jnp.stack([real_update, imag_update])

def reference(box_points, proxy_directions, point_order, neighbour_boxes, neighbour_places, pivot_inverse):
    ordered = jnp.take_along_axis(box_points, jnp.broadcast_to(point_order[:, None, :], box_points.shape), axis=2)
    shift_table = decode(neighbour_places)
    proxies = 0.5 + proxy_radius * proxy_directions

    def interp_one(which_box):
        own_points = ordered[which_box]
        near_points = ordered[neighbour_boxes[which_box]] + shift_table[which_box][:, :, None]
        near_points = jnp.transpose(near_points, (1, 0, 2)).reshape(3, NB * P_SIZE)
        targets = jnp.concatenate([proxies, near_points], axis=1)
        real_tile, imag_tile = helmholtz(targets, own_points)
        cross_terms = cross_products(real_tile.astype(jnp.bfloat16), imag_tile.astype(jnp.bfloat16), S)
        cholesky_factor = factor(cross_terms[:, :, :S])
        return apply_inverse(cholesky_factor, cross_terms[:, :, S:])
    interpolation = lax.map(interp_one, jnp.arange(BOXES, dtype=jnp.int32))

    def schur_box(which_box, running):
        own_points = ordered[which_box]
        near_points = ordered[neighbour_boxes[which_box]][:, :, :S] + shift_table[which_box][:, :, None]
        coefficients = interpolation[which_box]
        pivot_row = pivot_inverse[which_box]
        updates = jax.vmap(lambda points_one: pair_update(points_one, own_points, coefficients, pivot_row))(near_points)
        return running.at[neighbour_boxes[which_box]].add(updates)
    skeleton_update = lax.fori_loop(0, BOXES, schur_box, jnp.zeros((BOXES, 2, S, S), jnp.float32))
    return (interpolation, skeleton_update)
```

```python
import functools
import math

import jax
import jax.numpy as jnp
from jax import lax
from jax.experimental import pallas as pl
from jax.experimental.pallas import tpu as pltpu
from jax.sharding import PartitionSpec as P

S = 256

softening = 0.05
proxy_radius = 1.5
ridge_share = 0.05
highest = lax.Precision.HIGHEST
NBLK = 32
ROWS = 32

COS = (1.0, -19.73920440673828, 64.93911743164062, -85.45014190673828, 60.16762924194336,
       -25.967599868774414, 6.528658390045166)
SIN = (6.2831854820251465, -41.34170150756836, 81.60513305664062, -76.70301818847656,
       42.02592849731445, -14.899847030639648, 3.2381374835968018)

VMEM = pl.BlockSpec(memory_space=pltpu.VMEM)
SMEM = pl.BlockSpec(memory_space=pltpu.SMEM)


def params(**more):
    return pltpu.CompilerParams(vmem_limit_bytes=48 * 1024 * 1024, **more)


def horner(coefficients, z):
    total = jnp.full_like(z, coefficients[-1])
    for one in coefficients[-2::-1]:
        total = total * z + one
    return total


def kernel_values(tx, ty, tz, sx, sy, sz):
    dx = tx - sx
    dy = ty - sy
    dz = tz - sz
    square = dx * dx + dy * dy + dz * dz + softening * softening
    inverse = lax.rsqrt(square)
    inverse = inverse * (1.5 - 0.5 * square * inverse * inverse)
    turns = 2.0 * (square * inverse)
    part = turns - jnp.floor(turns + 0.5)
    z = part * part
    amplitude = inverse * (1.0 / (4.0 * math.pi))
    return amplitude * horner(COS, z), (amplitude * part) * horner(SIN, z)


def slot_of(nb_ref, where_ref, row, entry, box_count, box_total):
    owner_box = nb_ref[row, entry]
    step = owner_box // box_count - where_ref[0] + 1
    step = jnp.where(step < 0, step + box_total, step)
    step = jnp.where(step >= box_total, step - box_total, step)
    return step * box_count + owner_box % box_count


def dot_tn(a, b):
    return lax.dot_general(a, b, (((0,), (0,)), ((), ())), preferred_element_type=jnp.float32)


def tile_kernel(box_count, box_total, entries, where_ref, nb_ref, place_ref, points_ref, order_ref,
                proxy_ref, cross_ref, kern_ref, tcol, srow, tre, tim):
    count = points_ref.shape[2]
    proxies = proxy_ref.shape[1]
    box = where_ref[1]
    first = where_ref[2] * entries

    def ordered(slot):
        one_hot = (
            lax.broadcasted_iota(jnp.int32, (count, count), 0) == order_ref[slot, 0:1, :]
        ).astype(jnp.float32)
        return lax.dot_general(
            points_ref[slot], one_hot, (((1,), (0,)), ((), ())), precision=highest,
            preferred_element_type=jnp.float32,
        )

    axis_row = lax.broadcasted_iota(jnp.int32, (8, count), 0)
    srow[...] = ordered(box_count + box)
    tcol[0:proxies, 0:8] = jnp.transpose(0.5 + proxy_radius * proxy_ref[...])
    for k in range(entries):
        slot = slot_of(nb_ref, where_ref, box, first + k, box_count, box_total)
        code = place_ref[box, first + k]
        code = jnp.where(code >= 13, code + 1, code)
        shift = [(code // 9 - 1), (code // 3) % 3 - 1, code % 3 - 1]
        move = jnp.where(
            axis_row == 0,
            shift[0].astype(jnp.float32),
            jnp.where(axis_row == 1, shift[1].astype(jnp.float32), shift[2].astype(jnp.float32)),
        )
        start = proxies + k * count
        tcol[start:start + count, 0:8] = jnp.transpose(ordered(slot) + move)

    def strip(start):
        return kernel_values(
            tcol[pl.ds(start, ROWS), 0:1], tcol[pl.ds(start, ROWS), 1:2],
            tcol[pl.ds(start, ROWS), 2:3], srow[0:1, :], srow[1:2, :], srow[2:3, :],
        )

    def store(start, real, imag):
        tre[pl.ds(start, ROWS), :] = real.astype(jnp.bfloat16)
        tim[pl.ds(start, ROWS), :] = imag.astype(jnp.bfloat16)

    def plain(base, rows):
        @pl.loop(0, rows // ROWS)
        def _(i):
            start = pl.multiple_of(base + i * ROWS, ROWS)
            real, imag = strip(start)
            store(start, real, imag)

    def kept(base, k):
        @pl.loop(0, S // ROWS)
        def _(i):
            inner = pl.multiple_of(i * ROWS, ROWS)
            start = pl.multiple_of(base + inner, ROWS)
            real, imag = strip(start)
            store(start, real, imag)
            kern_ref[k, 0, pl.ds(inner, ROWS), :] = real
            kern_ref[k, 1, pl.ds(inner, ROWS), :] = imag

    plain(0, proxies)
    for k in range(entries):
        base = proxies + k * count
        kept(base, k)
        plain(base + S, count - S)
    left_re, left_im = tre[:, :S], tim[:, :S]
    cross_ref[0] = dot_tn(left_re, tre[...]) + dot_tn(left_im, tim[...])
    cross_ref[1] = dot_tn(left_re, tim[...]) - dot_tn(left_im, tre[...])


def exact(a, b, dims=((1,), (0,))):
    return lax.dot_general(a, b, (dims, ((), ())), precision=highest,
                           preferred_element_type=jnp.float32)


def solve_kernel(mine_ref, other_ref, x_ref, mat, low, high):
    n = x_ref.shape[1]
    wide = mine_ref.shape[2]
    nb = NBLK
    mat[...] = mine_ref[...] + other_ref[...]
    diagonal = lax.broadcasted_iota(jnp.int32, (n, n), 0) == lax.broadcasted_iota(
        jnp.int32, (n, n), 1
    )
    gram = mat[0, :, 0:n]
    ridge = ridge_share * jnp.sum(jnp.where(diagonal, gram, 0.0)) / n
    mat[0, :, 0:n] = gram + jnp.where(diagonal, ridge, 0.0)
    low[...] = jnp.zeros_like(low)
    high[...] = jnp.zeros_like(high)
    lane = lax.broadcasted_iota(jnp.int32, (nb, 128), 1)
    sub = lax.broadcasted_iota(jnp.int32, (nb, 128), 0)
    lane_all = lax.broadcasted_iota(jnp.int32, (n, 128), 1)
    for j in range(n // nb):
        rows = slice(j * nb, (j + 1) * nb)
        q = (j * nb) // 128 * 128
        back = (128 - (j * nb) % 128) % 128

        def turned(block, shift):
            return pltpu.roll(block, shift, 1) if shift else block

        block_re = mat[0, rows, q:q + 128]
        block_im = mat[1, rows, q:q + 128]
        re0, im0 = turned(block_re, back), turned(block_im, back)
        re1, im1 = turned(block_re, (back + nb) % 128), turned(block_im, (back + nb) % 128)
        zero = jnp.zeros_like(re0)
        m = jnp.where(lane < nb, re0, jnp.where(lane < 2 * nb, im1,
                                                jnp.where(lane - 2 * nb == sub, 1.0, zero)))
        w = jnp.where(lane < nb, -im0, jnp.where(lane < 2 * nb, re1,
                                                 jnp.where(lane - 3 * nb == sub, 1.0, zero)))
        for k in range(nb):
            col_re = m[:, k:k + 1]
            col_im = m[:, nb + k:nb + k + 1]
            scale = 1.0 / m[k:k + 1, k:k + 1]
            row_m = m[k:k + 1, :] * scale
            row_w = w[k:k + 1, :] * scale
            new_m = m - col_re * row_m - col_im * row_w
            new_w = w - col_re * row_w + col_im * row_m
            m = jnp.where(sub == k, row_m, new_m)
            w = jnp.where(sub == k, row_w, new_w)
        start = (j + 1) * nb // 128 * 128
        span = wide - start
        panel_re = mat[0, rows, start:]
        panel_im = mat[1, rows, start:]
        high[2 * nb:3 * nb, 0:span] = panel_re
        high[2 * nb:3 * nb, span:2 * span] = panel_im
        high[3 * nb:4 * nb, 0:span] = -panel_im
        high[3 * nb:4 * nb, span:2 * span] = panel_re
        solved = exact(m, high[:, 0:2 * span])
        low[0:nb, 0:2 * span] = solved
        low[nb:2 * nb, 0:span] = -solved[:, span:]
        low[nb:2 * nb, span:2 * span] = solved[:, 0:span]
        left = jnp.where(
            lane_all < nb,
            turned(mat[0, :, q:q + 128], back),
            jnp.where(lane_all < 2 * nb, turned(mat[1, :, q:q + 128], (back + nb) % 128), 0.0),
        )
        change = exact(left, low[:, 0:2 * span])
        mat[0, :, start:] = mat[0, :, start:] - change[:, 0:span]
        mat[1, :, start:] = mat[1, :, start:] - change[:, span:]
        mat[0, rows, start:] = solved[:, 0:span]
        mat[1, rows, start:] = solved[:, span:]
    x_ref[...] = mat[:, :, n:]


def update_kernel(box_count, box_total, entries, where_ref, nb_ref, kern_ref, x_ref, pivot_ref,
                  out_ref):
    n = x_ref.shape[1]
    box = where_ref[1]
    first = where_ref[2] * entries
    out_ref[...] = jnp.zeros_like(out_ref)
    xr, xi = x_ref[0], x_ref[1]
    qr, qi = pivot_ref[0:1, :], pivot_ref[1:2, :]
    nt = ((1,), (1,))
    for k in range(entries):
        slot = slot_of(nb_ref, where_ref, box, first + k, box_count, box_total)
        kr, ki = kern_ref[k, 0, :, 0:n], kern_ref[k, 1, :, 0:n]
        br = kern_ref[k, 0, :, n:] - (exact(kr, xr) - exact(ki, xi))
        bi = kern_ref[k, 1, :, n:] - (exact(kr, xi) + exact(ki, xr))
        wr = br * qr - bi * qi
        wi = br * qi + bi * qr
        out_ref[slot, 0] = out_ref[slot, 0] - (exact(wr, br, nt) - exact(wi, bi, nt))
        out_ref[slot, 1] = out_ref[slot, 1] - (exact(wr, bi, nt) + exact(wi, br, nt))


def ring(count, step):
    return [(i, (i + step) % count) for i in range(count)]


def on_device(
    box_points, proxy_directions, point_order, neighbour_boxes, neighbour_places, pivot_inverse
):
    box_count, _, point_count = box_points.shape
    col_count = lax.axis_size("col")
    box_total = lax.axis_size("box")
    col_index = lax.axis_index("col")
    box_index = lax.axis_index("box")
    group = col_count // box_count
    box = col_index // group
    part = col_index % group
    entries = neighbour_boxes.shape[1] // group
    width = pivot_inverse.shape[2]
    where = jnp.stack([box_index, box, part]).astype(jnp.int32)

    points = jnp.pad(box_points, ((0, 0), (0, 5), (0, 0)))
    order = point_order[:, None, :]

    def halo(block):
        low = lax.ppermute(block, "box", ring(box_total, 1))
        high = lax.ppermute(block, "box", ring(box_total, -1))
        return jnp.concatenate([low, block, high], axis=0)

    points = halo(points)
    order = halo(order)
    proxies = jnp.pad(proxy_directions, ((0, 5), (0, 0)))
    proxies = jnp.concatenate(
        [proxies] + [lax.ppermute(proxies, "col", ring(col_count, group * d))
                     for d in range(1, box_count)], axis=1)
    pieces = [pivot_inverse] + [lax.ppermute(pivot_inverse, "col", ring(col_count, d))
                                for d in range(1, col_count)]
    pieces = jnp.stack(pieces)
    pieces = pieces[(col_index - jnp.arange(col_count)) % col_count]
    pivots = jnp.moveaxis(lax.dynamic_index_in_dim(pieces, box, 1, keepdims=False), 0, 1)
    pivots = pivots.reshape(2, col_count * width)

    rows = proxies.shape[1] + entries * point_count
    cross, kern = pl.pallas_call(
        functools.partial(tile_kernel, box_count, box_total, entries),
        out_shape=(
            jax.ShapeDtypeStruct((2, S, point_count), jnp.float32),
            jax.ShapeDtypeStruct((entries, 2, S, point_count), jnp.float32),
        ),
        in_specs=[SMEM, SMEM, SMEM, VMEM, VMEM, VMEM],
        out_specs=(VMEM, VMEM),
        scratch_shapes=[
            pltpu.VMEM((rows, 128), jnp.float32),
            pltpu.VMEM((8, point_count), jnp.float32),
            pltpu.VMEM((rows, point_count), jnp.bfloat16),
            pltpu.VMEM((rows, point_count), jnp.bfloat16),
        ],
        compiler_params=params(),
    )(where, neighbour_boxes, neighbour_places, points, order, proxies)

    within = [(g * group + i, g * group + (i + 1) % group)
              for g in range(box_count) for i in range(group)]
    other = lax.ppermute(cross, "col", within)
    rest = point_count - S
    solved = pl.pallas_call(
        solve_kernel,
        out_shape=jax.ShapeDtypeStruct((2, S, rest), jnp.float32),
        in_specs=[VMEM, VMEM],
        out_specs=VMEM,
        scratch_shapes=[
            pltpu.VMEM((2, S, point_count), jnp.float32),
            pltpu.VMEM((128, 2 * point_count), jnp.float32),
            pltpu.VMEM((128, 2 * point_count), jnp.float32),
        ],
        compiler_params=params(),
    )(cross, other)

    mine = lax.dynamic_slice_in_dim(solved, col_index * width, width, 2)
    far = (col_index + group) % col_count
    sent = lax.dynamic_slice_in_dim(solved, far * width, width, 2)
    arrived = lax.ppermute(sent, "col", ring(col_count, group))
    interpolation = jnp.where(box == 0, jnp.stack([mine, arrived]), jnp.stack([arrived, mine]))

    buffer = pl.pallas_call(
        functools.partial(update_kernel, box_count, box_total, entries),
        out_shape=jax.ShapeDtypeStruct((3 * box_count, 2, S, S), jnp.float32),
        in_specs=[SMEM, SMEM, VMEM, VMEM, VMEM],
        out_specs=VMEM,
        compiler_params=params(),
    )(where, neighbour_boxes, kern, solved, pivots)

    reduced = lax.psum_scatter(buffer, "col", scatter_dimension=2, tiled=True)
    low = lax.ppermute(reduced[2 * box_count:], "box", ring(box_total, 1))
    high = lax.ppermute(reduced[:box_count], "box", ring(box_total, -1))
    skeleton_update = reduced[box_count:2 * box_count] + low + high
    return (interpolation, skeleton_update)


def solution(mesh):
    placed = (
        P("box", None, None),
        P(None, "col"),
        P("box", None),
        P("box", None),
        P("box", None),
        P("box", None, "col"),
    )
    return jax.shard_map(
        on_device,
        mesh=mesh,
        in_specs=placed,
        out_specs=(P("box", None, None, "col"), P("box", None, "col", None)),
        check_vma=False,
    )
```

```python
import functools
import math

import jax
import jax.numpy as jnp
from jax import lax
from jax.experimental import pallas as pl
from jax.experimental.pallas import tpu as pltpu
from jax.sharding import PartitionSpec as P

S = 256

softening = 0.05
proxy_radius = 1.5
ridge_share = 0.05
highest = lax.Precision.HIGHEST
NBLK = 32
ROWS = 32

COS = (1.0, -19.73920440673828, 64.93911743164062, -85.45014190673828, 60.16762924194336,
       -25.967599868774414, 6.528658390045166)
SIN = (6.2831854820251465, -41.34170150756836, 81.60513305664062, -76.70301818847656,
       42.02592849731445, -14.899847030639648, 3.2381374835968018)

VMEM = pl.BlockSpec(memory_space=pltpu.VMEM)
SMEM = pl.BlockSpec(memory_space=pltpu.SMEM)


def params(**more):
    return pltpu.CompilerParams(vmem_limit_bytes=48 * 1024 * 1024, **more)


def horner(coefficients, z):
    total = jnp.full_like(z, coefficients[-1])
    for one in coefficients[-2::-1]:
        total = total * z + one
    return total


def kernel_values(tx, ty, tz, sx, sy, sz):
    dx = tx - sx
    dy = ty - sy
    dz = tz - sz
    square = dx * dx + dy * dy + dz * dz + softening * softening
    inverse = lax.rsqrt(square)
    inverse = inverse * (1.5 - 0.5 * square * inverse * inverse)
    turns = 2.0 * (square * inverse)
    part = turns - jnp.floor(turns + 0.5)
    z = part * part
    amplitude = inverse * (1.0 / (4.0 * math.pi))
    return amplitude * horner(COS, z), (amplitude * part) * horner(SIN, z)


def slot_of(nb_ref, where_ref, row, entry, box_count, box_total):
    owner_box = nb_ref[row, entry]
    step = owner_box // box_count - where_ref[0] + 1
    step = jnp.where(step < 0, step + box_total, step)
    step = jnp.where(step >= box_total, step - box_total, step)
    return step * box_count + owner_box % box_count


def dot_tn(a, b):
    return lax.dot_general(a, b, (((0,), (0,)), ((), ())), preferred_element_type=jnp.float32)


def tile_kernel(box_count, box_total, entries, where_ref, nb_ref, place_ref, points_ref, order_ref,
                proxy_ref, cross_ref, kern_ref, tcol, srow, raw, tre, tim):
    count = points_ref.shape[3]
    share = proxy_ref.shape[2]
    proxies = box_count * share
    raw[...] = jnp.zeros_like(raw)
    box = where_ref[1]
    first = where_ref[2] * entries

    def ordered(slot):
        side, which = slot // box_count, slot % box_count
        one_hot = (
            lax.broadcasted_iota(jnp.int32, (count, count), 0)
            == order_ref[side, pl.ds(which, 1), :]
        ).astype(jnp.float32)
        raw[0:3, :] = points_ref[side, which]
        return lax.dot_general(
            raw[...], one_hot, (((1,), (0,)), ((), ())), precision=highest,
            preferred_element_type=jnp.float32,
        )

    axis_row = lax.broadcasted_iota(jnp.int32, (8, count), 0)
    srow[...] = ordered(box_count + box)
    for d in range(box_count):
        raw[0:3, 0:share] = 0.5 + proxy_radius * proxy_ref[d]
        tcol[d * share:(d + 1) * share, 0:8] = jnp.transpose(raw[:, 0:share])
    for k in range(entries):
        slot = slot_of(nb_ref, where_ref, box, first + k, box_count, box_total)
        code = place_ref[box, first + k]
        code = jnp.where(code >= 13, code + 1, code)
        shift = [(code // 9 - 1), (code // 3) % 3 - 1, code % 3 - 1]
        move = jnp.where(
            axis_row == 0,
            shift[0].astype(jnp.float32),
            jnp.where(axis_row == 1, shift[1].astype(jnp.float32), shift[2].astype(jnp.float32)),
        )
        start = proxies + k * count
        tcol[start:start + count, 0:8] = jnp.transpose(ordered(slot) + move)

    def strip(start):
        return kernel_values(
            tcol[pl.ds(start, ROWS), 0:1], tcol[pl.ds(start, ROWS), 1:2],
            tcol[pl.ds(start, ROWS), 2:3], srow[0:1, :], srow[1:2, :], srow[2:3, :],
        )

    def store(start, real, imag):
        tre[pl.ds(start, ROWS), :] = real.astype(jnp.bfloat16)
        tim[pl.ds(start, ROWS), :] = imag.astype(jnp.bfloat16)

    def plain(base, rows):
        @pl.loop(0, rows // ROWS)
        def _(i):
            start = pl.multiple_of(base + i * ROWS, ROWS)
            real, imag = strip(start)
            store(start, real, imag)

    def kept(base, k):
        @pl.loop(0, S // ROWS)
        def _(i):
            inner = pl.multiple_of(i * ROWS, ROWS)
            start = pl.multiple_of(base + inner, ROWS)
            real, imag = strip(start)
            store(start, real, imag)
            kern_ref[k, 0, pl.ds(inner, ROWS), :] = real
            kern_ref[k, 1, pl.ds(inner, ROWS), :] = imag

    plain(0, proxies)
    for k in range(entries):
        base = proxies + k * count
        kept(base, k)
        plain(base + S, count - S)
    left_re, left_im = tre[:, :S], tim[:, :S]
    cross_ref[0] = dot_tn(left_re, tre[...]) + dot_tn(left_im, tim[...])
    cross_ref[1] = dot_tn(left_re, tim[...]) - dot_tn(left_im, tre[...])


def exact(a, b, dims=((1,), (0,))):
    return lax.dot_general(a, b, (dims, ((), ())), precision=highest,
                           preferred_element_type=jnp.float32)


def solve_kernel(mine_ref, other_ref, x_ref, mat, low, high):
    n = x_ref.shape[1]
    wide = mine_ref.shape[2]
    nb = NBLK
    mat[...] = mine_ref[...] + other_ref[...]
    diagonal = lax.broadcasted_iota(jnp.int32, (n, n), 0) == lax.broadcasted_iota(
        jnp.int32, (n, n), 1
    )
    gram = mat[0, :, 0:n]
    ridge = ridge_share * jnp.sum(jnp.where(diagonal, gram, 0.0)) / n
    mat[0, :, 0:n] = gram + jnp.where(diagonal, ridge, 0.0)
    low[...] = jnp.zeros_like(low)
    high[...] = jnp.zeros_like(high)
    lane = lax.broadcasted_iota(jnp.int32, (nb, 128), 1)
    sub = lax.broadcasted_iota(jnp.int32, (nb, 128), 0)
    lane_all = lax.broadcasted_iota(jnp.int32, (n, 128), 1)
    for j in range(n // nb):
        rows = slice(j * nb, (j + 1) * nb)
        q = (j * nb) // 128 * 128
        back = (128 - (j * nb) % 128) % 128

        def turned(block, shift):
            return pltpu.roll(block, shift, 1) if shift else block

        block_re = mat[0, rows, q:q + 128]
        block_im = mat[1, rows, q:q + 128]
        re0, im0 = turned(block_re, back), turned(block_im, back)
        re1, im1 = turned(block_re, (back + nb) % 128), turned(block_im, (back + nb) % 128)
        zero = jnp.zeros_like(re0)
        m = jnp.where(lane < nb, re0, jnp.where(lane < 2 * nb, im1,
                                                jnp.where(lane - 2 * nb == sub, 1.0, zero)))
        w = jnp.where(lane < nb, -im0, jnp.where(lane < 2 * nb, re1,
                                                 jnp.where(lane - 3 * nb == sub, 1.0, zero)))
        for k in range(nb):
            col_re = m[:, k:k + 1]
            col_im = m[:, nb + k:nb + k + 1]
            scale = 1.0 / m[k:k + 1, k:k + 1]
            row_m = m[k:k + 1, :] * scale
            row_w = w[k:k + 1, :] * scale
            new_m = m - col_re * row_m - col_im * row_w
            new_w = w - col_re * row_w + col_im * row_m
            m = jnp.where(sub == k, row_m, new_m)
            w = jnp.where(sub == k, row_w, new_w)
        start = (j + 1) * nb // 128 * 128
        span = wide - start
        panel_re = mat[0, rows, start:]
        panel_im = mat[1, rows, start:]
        high[2 * nb:3 * nb, 0:span] = panel_re
        high[2 * nb:3 * nb, span:2 * span] = panel_im
        high[3 * nb:4 * nb, 0:span] = -panel_im
        high[3 * nb:4 * nb, span:2 * span] = panel_re
        solved = exact(m, high[:, 0:2 * span])
        low[0:nb, 0:2 * span] = solved
        low[nb:2 * nb, 0:span] = -solved[:, span:]
        low[nb:2 * nb, span:2 * span] = solved[:, 0:span]
        left = jnp.where(
            lane_all < nb,
            turned(mat[0, :, q:q + 128], back),
            jnp.where(lane_all < 2 * nb, turned(mat[1, :, q:q + 128], (back + nb) % 128), 0.0),
        )
        change = exact(left, low[:, 0:2 * span])
        mat[0, :, start:] = mat[0, :, start:] - change[:, 0:span]
        mat[1, :, start:] = mat[1, :, start:] - change[:, span:]
        mat[0, rows, start:] = solved[:, 0:span]
        mat[1, rows, start:] = solved[:, span:]
    x_ref[...] = mat[:, :, n:]


def update_kernel(box_count, box_total, entries, where_ref, nb_ref, kern_ref, x_ref, pivot_ref,
                  out_ref):
    n = x_ref.shape[1]
    box = where_ref[1]
    first = where_ref[2] * entries
    out_ref[...] = jnp.zeros_like(out_ref)
    xr, xi = x_ref[0], x_ref[1]
    pieces = range(pivot_ref.shape[0])
    qr = jnp.concatenate([pivot_ref[c, box, 0:1, :] for c in pieces], axis=1)
    qi = jnp.concatenate([pivot_ref[c, box, 1:2, :] for c in pieces], axis=1)
    nt = ((1,), (1,))
    for k in range(entries):
        slot = slot_of(nb_ref, where_ref, box, first + k, box_count, box_total)
        kr, ki = kern_ref[k, 0, :, 0:n], kern_ref[k, 1, :, 0:n]
        br = kern_ref[k, 0, :, n:] - (exact(kr, xr) - exact(ki, xi))
        bi = kern_ref[k, 1, :, n:] - (exact(kr, xi) + exact(ki, xr))
        wr = br * qr - bi * qi
        wi = br * qi + bi * qr
        out_ref[slot, 0] = out_ref[slot, 0] - (exact(wr, br, nt) - exact(wi, bi, nt))
        out_ref[slot, 1] = out_ref[slot, 1] - (exact(wr, bi, nt) + exact(wi, br, nt))


MESH = pl.DeviceIdType.MESH


def meet(peers):
    barrier = pltpu.get_barrier_semaphore()
    for peer in peers:
        pl.semaphore_signal(barrier, inc=1, device_id=peer, device_id_type=MESH)
    pl.semaphore_wait(barrier, len(peers))


def exchange_kernel(box_total, col_count, group, points_ref, order_ref, proxy_ref, pivot_ref,
                    points_out, order_out, proxy_out, pivot_out, send, recv):
    me = lax.axis_index("col")
    place = lax.axis_index("box")
    after = {"box": lax.rem(place + 1, box_total)}
    before = {"box": lax.rem(place + box_total - 1, box_total)}
    peers = [{"col": lax.rem(me + d, col_count)} for d in range(1, col_count)]
    meet([before, after] + peers)
    jobs = [
        (points_ref, points_out.at[0], after),
        (points_ref, points_out.at[2], before),
        (order_ref, order_out.at[0], after),
        (order_ref, order_out.at[2], before),
    ]
    for d in range(1, col_count):
        jobs.append((pivot_ref, pivot_out.at[me], peers[d - 1]))
        if d % group == 0:
            jobs.append((proxy_ref, proxy_out.at[d // group], peers[d - 1]))
    copies = []
    for i, (source, target, peer) in enumerate(jobs):
        copy = pltpu.make_async_remote_copy(
            src_ref=source, dst_ref=target, send_sem=send.at[i], recv_sem=recv.at[i],
            device_id=peer, device_id_type=MESH)
        copy.start()
        copies.append(copy)
    points_out[1] = points_ref[...]
    order_out[1] = order_ref[...]
    proxy_out[0] = proxy_ref[...]
    pivot_out[me] = pivot_ref[...]
    for copy in copies:
        copy.wait()


def reduce_kernel(box_total, col_count, group, buf_ref, out_ref, pair_in, cross_out, cross_in,
                  held, box_in, send, recv):
    me = lax.axis_index("col")
    place = lax.axis_index("box")
    partner = me + 1 - 2 * lax.rem(me, 2)
    across = lax.rem(me + group, col_count)
    far = lax.rem(partner + group, col_count)
    near_id, far_id = {"col": partner}, {"col": across}
    after = {"box": lax.rem(place + 1, box_total)}
    before = {"box": lax.rem(place + box_total - 1, box_total)}
    meet([near_id, far_id, before, after])
    width = out_ref.shape[0]

    def copy(index, source, target, peer):
        one = pltpu.make_async_remote_copy(
            src_ref=source, dst_ref=target, send_sem=send.at[index], recv_sem=recv.at[index],
            device_id=peer, device_id_type=MESH)
        one.start()
        return one

    turn = (0, 2, 1)
    pairs = {}
    for kind, block in ((0, far), (1, partner)):
        for g in turn:
            source = buf_ref.at[pl.ds(g * width, width), :, block]
            pairs[g, kind] = copy(2 * g + kind, source, pair_in.at[g, kind], near_id)
    cross = {}
    for g in turn:
        pairs[g, 0].wait()
        cross_out[g] = buf_ref[g * width:(g + 1) * width, :, across] + pair_in[g, 0]
        cross[g] = copy(6 + g, cross_out.at[g], cross_in.at[g], far_id)
    for g in turn:
        pairs[g, 1].wait()
        held[g] = buf_ref[g * width:(g + 1) * width, :, me] + pair_in[g, 1]
    moves = []
    for side, (g, peer) in enumerate(((0, before), (2, after))):
        cross[g].wait()
        held[g] = held[g] + cross_in[g]
        moves.append(copy(9 + side, held.at[g], box_in.at[side], peer))
    cross[1].wait()
    total = held[1] + cross_in[1]
    moves[0].wait()
    held[1] = total + box_in[0]
    moves[1].wait()
    out_ref[...] = held[1] + box_in[1]


def ring(count, step):
    return [(i, (i + step) % count) for i in range(count)]


def on_device(
    box_points, proxy_directions, point_order, neighbour_boxes, neighbour_places, pivot_inverse
):
    box_count, _, point_count = box_points.shape
    col_count = lax.axis_size("col")
    box_total = lax.axis_size("box")
    col_index = lax.axis_index("col")
    box_index = lax.axis_index("box")
    group = col_count // box_count
    box = col_index // group
    part = col_index % group
    entries = neighbour_boxes.shape[1] // group
    width = pivot_inverse.shape[2]
    where = jnp.stack([box_index, box, part]).astype(jnp.int32)

    jobs = 4 + col_count - 1 + box_count - 1
    points, order, proxies, pivots = pl.pallas_call(
        functools.partial(exchange_kernel, box_total, col_count, group),
        out_shape=(
            jax.ShapeDtypeStruct((3,) + box_points.shape, jnp.float32),
            jax.ShapeDtypeStruct((3,) + point_order.shape, jnp.int32),
            jax.ShapeDtypeStruct((box_count,) + proxy_directions.shape, jnp.float32),
            jax.ShapeDtypeStruct((col_count,) + pivot_inverse.shape, jnp.float32),
        ),
        in_specs=[VMEM] * 4,
        out_specs=(VMEM,) * 4,
        scratch_shapes=[pltpu.SemaphoreType.DMA((jobs,)), pltpu.SemaphoreType.DMA((jobs,))],
        compiler_params=params(collective_id=0, has_side_effects=True),
    )(box_points, point_order, proxy_directions, pivot_inverse)

    share = proxy_directions.shape[1]
    rows = box_count * share + entries * point_count
    cross, kern = pl.pallas_call(
        functools.partial(tile_kernel, box_count, box_total, entries),
        out_shape=(
            jax.ShapeDtypeStruct((2, S, point_count), jnp.float32),
            jax.ShapeDtypeStruct((entries, 2, S, point_count), jnp.float32),
        ),
        in_specs=[SMEM, SMEM, SMEM, VMEM, VMEM, VMEM],
        out_specs=(VMEM, VMEM),
        scratch_shapes=[
            pltpu.VMEM((rows, 128), jnp.float32),
            pltpu.VMEM((8, point_count), jnp.float32),
            pltpu.VMEM((8, point_count), jnp.float32),
            pltpu.VMEM((rows, point_count), jnp.bfloat16),
            pltpu.VMEM((rows, point_count), jnp.bfloat16),
        ],
        compiler_params=params(),
    )(where, neighbour_boxes, neighbour_places, points, order, proxies)

    within = [(g * group + i, g * group + (i + 1) % group)
              for g in range(box_count) for i in range(group)]
    other = lax.ppermute(cross, "col", within)
    rest = point_count - S
    solved = pl.pallas_call(
        solve_kernel,
        out_shape=jax.ShapeDtypeStruct((2, S, rest), jnp.float32),
        in_specs=[VMEM, VMEM],
        out_specs=VMEM,
        scratch_shapes=[
            pltpu.VMEM((2, S, point_count), jnp.float32),
            pltpu.VMEM((128, 2 * point_count), jnp.float32),
            pltpu.VMEM((128, 2 * point_count), jnp.float32),
        ],
        compiler_params=params(),
    )(cross, other)

    mine = lax.dynamic_slice_in_dim(solved, col_index * width, width, 2)
    far = (col_index + group) % col_count
    sent = lax.dynamic_slice_in_dim(solved, far * width, width, 2)
    arrived = lax.ppermute(sent, "col", ring(col_count, group))
    interpolation = jnp.where(box == 0, jnp.stack([mine, arrived]), jnp.stack([arrived, mine]))

    buffer = pl.pallas_call(
        functools.partial(update_kernel, box_count, box_total, entries),
        out_shape=jax.ShapeDtypeStruct((3 * box_count, 2, S, S), jnp.float32),
        in_specs=[SMEM, SMEM, VMEM, VMEM, VMEM],
        out_specs=VMEM,
        compiler_params=params(),
    )(where, neighbour_boxes, kern, solved, pivots)

    strip = S // col_count
    block = (box_count, 2, strip, S)
    skeleton_update = pl.pallas_call(
        functools.partial(reduce_kernel, box_total, col_count, group),
        out_shape=jax.ShapeDtypeStruct(block, jnp.float32),
        in_specs=[VMEM],
        out_specs=VMEM,
        scratch_shapes=[
            pltpu.VMEM((3, 2) + block, jnp.float32),
            pltpu.VMEM((3,) + block, jnp.float32),
            pltpu.VMEM((3,) + block, jnp.float32),
            pltpu.VMEM((3,) + block, jnp.float32),
            pltpu.VMEM((2,) + block, jnp.float32),
            pltpu.SemaphoreType.DMA((11,)),
            pltpu.SemaphoreType.DMA((11,)),
        ],
        compiler_params=params(collective_id=1, has_side_effects=True),
    )(buffer.reshape(3 * box_count, 2, col_count, strip, S))
    return (interpolation, skeleton_update)


def solution(mesh):
    placed = (
        P("box", None, None),
        P(None, "col"),
        P("box", None),
        P("box", None),
        P("box", None),
        P("box", None, "col"),
    )
    return jax.shard_map(
        on_device,
        mesh=mesh,
        in_specs=placed,
        out_specs=(P("box", None, None, "col"), P("box", None, "col", None)),
        check_vma=False,
    )
```

```python
import functools
import math

import jax
import jax.numpy as jnp
from jax import lax
from jax.experimental import pallas as pl
from jax.experimental.pallas import tpu as pltpu
from jax.sharding import PartitionSpec as P

S = 256

softening = 0.05
proxy_radius = 1.5
ridge_share = 0.05
highest = lax.Precision.HIGHEST
NBLK = 32
ROWS = 32

COS = (1.4142135381698608, -6.978850841522217, 5.739460468292236, -1.883557915687561, 0.3106880187988281)
SIN = (4.442883014678955, -7.308245658874512, 3.606354236602783, -0.8461116552352905, 0.1098245158791542)

VMEM = pl.BlockSpec(memory_space=pltpu.VMEM)
SMEM = pl.BlockSpec(memory_space=pltpu.SMEM)


def params(**more):
    return pltpu.CompilerParams(vmem_limit_bytes=48 * 1024 * 1024, **more)


def horner(coefficients, z):
    total = jnp.full_like(z, coefficients[-1])
    for one in coefficients[-2::-1]:
        total = total * z + one
    return total


def kernel_values(tx, ty, tz, sx, sy, sz):
    dx = tx - sx
    dy = ty - sy
    dz = tz - sz
    square = (dx * dx + dy * dy) + (dz * dz + 4.0 * softening * softening)
    inverse = lax.rsqrt(square)
    turns = square * inverse
    part = turns - jnp.floor(turns + 0.5)
    z = part * part
    amplitude = inverse * (1.0 / (2.0 * math.pi))
    sine = part * horner(SIN, z)
    scaled = amplitude * sine
    return amplitude - scaled * sine, scaled * horner(COS, z)


def slot_of(nb_ref, where_ref, row, entry, box_count, box_total):
    owner_box = nb_ref[row, entry]
    step = owner_box // box_count - where_ref[0] + 1
    step = jnp.where(step < 0, step + box_total, step)
    step = jnp.where(step >= box_total, step - box_total, step)
    return step * box_count + owner_box % box_count


def dot_tn(a, b):
    return lax.dot_general(a, b, (((0,), (0,)), ((), ())), preferred_element_type=jnp.float32)


def tile_kernel(box_count, box_total, entries, where_ref, nb_ref, place_ref, points_ref, order_ref,
                proxy_ref, cross_ref, kern_ref, tcol, srow, raw, tre, tim):
    count = points_ref.shape[3]
    share = proxy_ref.shape[2]
    proxies = box_count * share
    raw[...] = jnp.zeros_like(raw)
    box = where_ref[1]
    first = where_ref[2] * entries

    def ordered(slot):
        side, which = slot // box_count, slot % box_count
        one_hot = (
            lax.broadcasted_iota(jnp.int32, (count, count), 0)
            == order_ref[side, pl.ds(which, 1), :]
        ).astype(jnp.float32)
        raw[0:3, :] = points_ref[side, which]
        return lax.dot_general(
            raw[...], one_hot, (((1,), (0,)), ((), ())), precision=highest,
            preferred_element_type=jnp.float32,
        )

    axis_row = lax.broadcasted_iota(jnp.int32, (8, count), 0)
    srow[...] = 2.0 * ordered(box_count + box)
    for d in range(box_count):
        raw[0:3, 0:share] = 2.0 * (0.5 + proxy_radius * proxy_ref[d])
        tcol[d * share:(d + 1) * share, 0:8] = jnp.transpose(raw[:, 0:share])
    for k in range(entries):
        slot = slot_of(nb_ref, where_ref, box, first + k, box_count, box_total)
        code = place_ref[box, first + k]
        code = jnp.where(code >= 13, code + 1, code)
        shift = [(code // 9 - 1), (code // 3) % 3 - 1, code % 3 - 1]
        move = jnp.where(
            axis_row == 0,
            shift[0].astype(jnp.float32),
            jnp.where(axis_row == 1, shift[1].astype(jnp.float32), shift[2].astype(jnp.float32)),
        )
        start = proxies + k * count
        tcol[start:start + count, 0:8] = jnp.transpose(2.0 * (ordered(slot) + move))

    def strip(start):
        return kernel_values(
            tcol[pl.ds(start, ROWS), 0:1], tcol[pl.ds(start, ROWS), 1:2],
            tcol[pl.ds(start, ROWS), 2:3], srow[0:1, :], srow[1:2, :], srow[2:3, :],
        )

    def store(start, real, imag):
        tre[pl.ds(start, ROWS), :] = real.astype(jnp.bfloat16)
        tim[pl.ds(start, ROWS), :] = imag.astype(jnp.bfloat16)

    def plain(base, rows):
        @pl.loop(0, rows // ROWS)
        def _(i):
            start = pl.multiple_of(base + i * ROWS, ROWS)
            real, imag = strip(start)
            store(start, real, imag)

    def kept(base, k):
        @pl.loop(0, S // ROWS)
        def _(i):
            inner = pl.multiple_of(i * ROWS, ROWS)
            start = pl.multiple_of(base + inner, ROWS)
            real, imag = strip(start)
            store(start, real, imag)
            kern_ref[k, 0, pl.ds(inner, ROWS), :] = real
            kern_ref[k, 1, pl.ds(inner, ROWS), :] = imag

    plain(0, proxies)
    for k in range(entries):
        base = proxies + k * count
        kept(base, k)
        plain(base + S, count - S)
    left_re, left_im = tre[:, :S], tim[:, :S]
    cross_ref[0] = dot_tn(left_re, tre[...]) + dot_tn(left_im, tim[...])
    cross_ref[1] = dot_tn(left_re, tim[...]) - dot_tn(left_im, tre[...])


def exact(a, b, dims=((1,), (0,))):
    return lax.dot_general(a, b, (dims, ((), ())), precision=highest,
                           preferred_element_type=jnp.float32)


def solve_kernel(mine_ref, other_ref, x_ref, mat, low, high):
    n = x_ref.shape[1]
    wide = mine_ref.shape[2]
    nb = NBLK
    mat[...] = mine_ref[...] + other_ref[...]
    diagonal = lax.broadcasted_iota(jnp.int32, (n, n), 0) == lax.broadcasted_iota(
        jnp.int32, (n, n), 1
    )
    gram = mat[0, :, 0:n]
    ridge = ridge_share * jnp.sum(jnp.where(diagonal, gram, 0.0)) / n
    mat[0, :, 0:n] = gram + jnp.where(diagonal, ridge, 0.0)
    low[...] = jnp.zeros_like(low)
    high[...] = jnp.zeros_like(high)
    lane = lax.broadcasted_iota(jnp.int32, (nb, 128), 1)
    sub = lax.broadcasted_iota(jnp.int32, (nb, 128), 0)
    lane_all = lax.broadcasted_iota(jnp.int32, (n, 128), 1)

    def turned(block, shift):
        return pltpu.roll(block, shift, 1) if shift else block

    def inverse(block_re, block_im, back):
        re0, im0 = turned(block_re, back), turned(block_im, back)
        re1, im1 = turned(block_re, (back + nb) % 128), turned(block_im, (back + nb) % 128)
        zero = jnp.zeros_like(re0)
        m = jnp.where(lane < nb, re0, jnp.where(lane < 2 * nb, im1,
                                                jnp.where(lane - 2 * nb == sub, 1.0, zero)))
        w = jnp.where(lane < nb, -im0, jnp.where(lane < 2 * nb, re1,
                                                 jnp.where(lane - 3 * nb == sub, 1.0, zero)))

        def spread(block, k):
            return jnp.broadcast_to(block[:, k:k + 1], (nb, 128))

        for k in range(0, nb, 2):
            p0, p1 = spread(m, k), spread(m, k + 1)
            s0, s1 = spread(m, nb + k), spread(m, nb + k + 1)
            a, d = p0[k:k + 1], p1[k + 1:k + 2]
            br, bi = p1[k:k + 1], s1[k:k + 1]
            scale = 1.0 / (a * d - (br * br + bi * bi))
            m0, m1, w0, w1 = m[k:k + 1], m[k + 1:k + 2], w[k:k + 1], w[k + 1:k + 2]
            row_m0 = (d * m0 - (br * m1 + bi * w1)) * scale
            row_w0 = (d * w0 - (br * w1 - bi * m1)) * scale
            row_m1 = (a * m1 - (br * m0 - bi * w0)) * scale
            row_w1 = (a * w1 - (br * w0 + bi * m0)) * scale
            new_m = m - ((p0 * row_m0 + s0 * row_w0) + (p1 * row_m1 + s1 * row_w1))
            new_w = w - ((p0 * row_w0 - s0 * row_m0) + (p1 * row_w1 - s1 * row_m1))
            m = jnp.where(sub == k, row_m0, jnp.where(sub == k + 1, row_m1, new_m))
            w = jnp.where(sub == k, row_w0, jnp.where(sub == k + 1, row_w1, new_w))
        return m

    m = inverse(mat[0, 0:nb, 0:128], mat[1, 0:nb, 0:128], 0)
    for j in range(n // nb):
        rows = slice(j * nb, (j + 1) * nb)
        after = slice((j + 1) * nb, (j + 2) * nb)
        q = (j * nb) // 128 * 128
        back = (128 - (j * nb) % 128) % 128
        start = (j + 1) * nb // 128 * 128
        span = wide - start
        panel_re = mat[0, rows, start:]
        panel_im = mat[1, rows, start:]
        high[2 * nb:3 * nb, 0:span] = panel_re
        high[2 * nb:3 * nb, span:2 * span] = panel_im
        high[3 * nb:4 * nb, 0:span] = -panel_im
        high[3 * nb:4 * nb, span:2 * span] = panel_re
        solved = exact(m, high[:, 0:2 * span])
        low[0:nb, 0:2 * span] = solved
        low[nb:2 * nb, 0:span] = -solved[:, span:]
        low[nb:2 * nb, span:2 * span] = solved[:, 0:span]
        left = jnp.where(
            lane_all < nb,
            turned(mat[0, :, q:q + 128], back),
            jnp.where(lane_all < 2 * nb, turned(mat[1, :, q:q + 128], (back + nb) % 128), 0.0),
        )
        if (j + 1) * nb < n:
            ahead = left[after]
            next_re = mat[0, after, start:start + 128] - exact(ahead, low[:, 0:128])
            next_im = mat[1, after, start:start + 128] - exact(ahead, low[:, span:span + 128])
            m = inverse(next_re, next_im, (128 - ((j + 1) * nb) % 128) % 128)
        change = exact(left, low[:, 0:2 * span])
        mat[0, :, start:] = mat[0, :, start:] - change[:, 0:span]
        mat[1, :, start:] = mat[1, :, start:] - change[:, span:]
        mat[0, rows, start:] = solved[:, 0:span]
        mat[1, rows, start:] = solved[:, span:]
    x_ref[...] = mat[:, :, n:]


def split(x):
    high = x.astype(jnp.bfloat16)
    return high, (x - high.astype(jnp.float32)).astype(jnp.bfloat16)


def threefold(a, b, dims=((1,), (0,))):
    def one(x, y):
        return lax.dot_general(x, y, (dims, ((), ())), preferred_element_type=jnp.float32)

    return one(a[0], b[0]) + (one(a[0], b[1]) + one(a[1], b[0]))


def update_kernel(box_count, box_total, entries, where_ref, nb_ref, kern_ref, x_ref, pivot_ref,
                  out_ref):
    n = x_ref.shape[1]
    box = where_ref[1]
    first = where_ref[2] * entries
    out_ref[...] = jnp.zeros_like(out_ref)
    xr, xi = x_ref[0], x_ref[1]
    right = split(jnp.concatenate(
        [jnp.concatenate([xr, xi], axis=1), jnp.concatenate([-xi, xr], axis=1)], axis=0))
    pieces = range(pivot_ref.shape[0])
    qr = jnp.concatenate([pivot_ref[c, box, 0:1, :] for c in pieces], axis=1)
    qi = jnp.concatenate([pivot_ref[c, box, 1:2, :] for c in pieces], axis=1)
    nt = ((1,), (1,))
    for k in range(entries):
        slot = slot_of(nb_ref, where_ref, box, first + k, box_count, box_total)
        left = split(jnp.concatenate([kern_ref[k, 0, :, 0:n], kern_ref[k, 1, :, 0:n]], axis=1))
        both = threefold(left, right)
        br = kern_ref[k, 0, :, n:] - both[:, 0:n]
        bi = kern_ref[k, 1, :, n:] - both[:, n:]
        wr = split(br * qr - bi * qi)
        wi = split(br * qi + bi * qr)
        sr, si = split(br), split(bi)
        out_ref[slot, 0] = out_ref[slot, 0] - (threefold(wr, sr, nt) - threefold(wi, si, nt))
        out_ref[slot, 1] = out_ref[slot, 1] - (threefold(wr, si, nt) + threefold(wi, sr, nt))


MESH = pl.DeviceIdType.MESH


def meet(peers):
    barrier = pltpu.get_barrier_semaphore()
    for peer in peers:
        pl.semaphore_signal(barrier, inc=1, device_id=peer, device_id_type=MESH)
    pl.semaphore_wait(barrier, len(peers))


def exchange_kernel(box_total, col_count, group, points_ref, order_ref, proxy_ref, pivot_ref,
                    points_out, order_out, proxy_out, pivot_out, send, recv, local):
    me = lax.axis_index("col")
    place = lax.axis_index("box")
    after = {"box": lax.rem(place + 1, box_total)}
    before = {"box": lax.rem(place + box_total - 1, box_total)}
    peers = [{"col": lax.rem(me + d, col_count)} for d in range(1, col_count)]
    meet([before, after] + peers)
    jobs = [
        (points_ref, points_out.at[0], after),
        (points_ref, points_out.at[2], before),
        (order_ref, order_out.at[0], after),
        (order_ref, order_out.at[2], before),
    ]
    for d in range(1, col_count):
        jobs.append((pivot_ref, pivot_out.at[me], peers[d - 1]))
        if d % group == 0:
            jobs.append((proxy_ref, proxy_out.at[d // group], peers[d - 1]))
    copies = []
    for i, (source, target, peer) in enumerate(jobs):
        copy = pltpu.make_async_remote_copy(
            src_ref=source, dst_ref=target, send_sem=send.at[i], recv_sem=recv.at[i],
            device_id=peer, device_id_type=MESH)
        copy.start()
        copies.append(copy)
    own = ((points_ref, points_out.at[1]), (order_ref, order_out.at[1]),
           (proxy_ref, proxy_out.at[0]), (pivot_ref, pivot_out.at[me]))
    for i, (source, target) in enumerate(own):
        copy = pltpu.make_async_copy(source, target, local.at[i])
        copy.start()
        copies.append(copy)
    for copy in copies:
        copy.wait()


def reduce_kernel(box_total, col_count, group, buf_ref, out_ref, pair_in, cross_out, cross_in,
                  held, box_in, send, recv):
    me = lax.axis_index("col")
    place = lax.axis_index("box")
    partner = me + 1 - 2 * lax.rem(me, 2)
    across = lax.rem(me + group, col_count)
    far = lax.rem(partner + group, col_count)
    near_id, far_id = {"col": partner}, {"col": across}
    after = {"box": lax.rem(place + 1, box_total)}
    before = {"box": lax.rem(place + box_total - 1, box_total)}
    meet([near_id, far_id, before, after])
    width = out_ref.shape[0]

    def copy(index, source, target, peer):
        one = pltpu.make_async_remote_copy(
            src_ref=source, dst_ref=target, send_sem=send.at[index], recv_sem=recv.at[index],
            device_id=peer, device_id_type=MESH)
        one.start()
        return one

    turn = (0, 2, 1)
    pairs = {}
    for kind, block in ((0, far), (1, partner)):
        for g in turn:
            source = buf_ref.at[pl.ds(g * width, width), :, block]
            pairs[g, kind] = copy(2 * g + kind, source, pair_in.at[g, kind], near_id)
    cross = {}
    for g in turn:
        pairs[g, 0].wait()
        cross_out[g] = buf_ref[g * width:(g + 1) * width, :, across] + pair_in[g, 0]
        cross[g] = copy(6 + g, cross_out.at[g], cross_in.at[g], far_id)
    for g in turn:
        pairs[g, 1].wait()
        held[g] = buf_ref[g * width:(g + 1) * width, :, me] + pair_in[g, 1]
    moves = []
    for side, (g, peer) in enumerate(((0, before), (2, after))):
        cross[g].wait()
        held[g] = held[g] + cross_in[g]
        moves.append(copy(9 + side, held.at[g], box_in.at[side], peer))
    cross[1].wait()
    total = held[1] + cross_in[1]
    moves[0].wait()
    held[1] = total + box_in[0]
    moves[1].wait()
    out_ref[...] = held[1] + box_in[1]


def ring(count, step):
    return [(i, (i + step) % count) for i in range(count)]


def on_device(
    box_points, proxy_directions, point_order, neighbour_boxes, neighbour_places, pivot_inverse
):
    box_count, _, point_count = box_points.shape
    col_count = lax.axis_size("col")
    box_total = lax.axis_size("box")
    col_index = lax.axis_index("col")
    box_index = lax.axis_index("box")
    group = col_count // box_count
    box = col_index // group
    part = col_index % group
    entries = neighbour_boxes.shape[1] // group
    width = pivot_inverse.shape[2]
    where = jnp.stack([box_index, box, part]).astype(jnp.int32)

    jobs = 4 + col_count - 1 + box_count - 1
    points, order, proxies, pivots = pl.pallas_call(
        functools.partial(exchange_kernel, box_total, col_count, group),
        out_shape=(
            jax.ShapeDtypeStruct((3,) + box_points.shape, jnp.float32),
            jax.ShapeDtypeStruct((3,) + point_order.shape, jnp.int32),
            jax.ShapeDtypeStruct((box_count,) + proxy_directions.shape, jnp.float32),
            jax.ShapeDtypeStruct((col_count,) + pivot_inverse.shape, jnp.float32),
        ),
        in_specs=[pl.BlockSpec(memory_space=pl.ANY)] * 4,
        out_specs=(VMEM,) * 4,
        scratch_shapes=[pltpu.SemaphoreType.DMA((jobs,)), pltpu.SemaphoreType.DMA((jobs,)),
                        pltpu.SemaphoreType.DMA((4,))],
        compiler_params=params(collective_id=0, has_side_effects=True),
    )(box_points, point_order, proxy_directions, pivot_inverse)

    share = proxy_directions.shape[1]
    rows = box_count * share + entries * point_count
    cross, kern = pl.pallas_call(
        functools.partial(tile_kernel, box_count, box_total, entries),
        out_shape=(
            jax.ShapeDtypeStruct((2, S, point_count), jnp.float32),
            jax.ShapeDtypeStruct((entries, 2, S, point_count), jnp.float32),
        ),
        in_specs=[SMEM, SMEM, SMEM, VMEM, VMEM, VMEM],
        out_specs=(VMEM, VMEM),
        scratch_shapes=[
            pltpu.VMEM((rows, 128), jnp.float32),
            pltpu.VMEM((8, point_count), jnp.float32),
            pltpu.VMEM((8, point_count), jnp.float32),
            pltpu.VMEM((rows, point_count), jnp.bfloat16),
            pltpu.VMEM((rows, point_count), jnp.bfloat16),
        ],
        compiler_params=params(),
    )(where, neighbour_boxes, neighbour_places, points, order, proxies)

    within = [(g * group + i, g * group + (i + 1) % group)
              for g in range(box_count) for i in range(group)]
    other = lax.ppermute(cross, "col", within)
    rest = point_count - S
    solved = pl.pallas_call(
        solve_kernel,
        out_shape=jax.ShapeDtypeStruct((2, S, rest), jnp.float32),
        in_specs=[VMEM, VMEM],
        out_specs=VMEM,
        scratch_shapes=[
            pltpu.VMEM((2, S, point_count), jnp.float32),
            pltpu.VMEM((128, 2 * point_count), jnp.float32),
            pltpu.VMEM((128, 2 * point_count), jnp.float32),
        ],
        compiler_params=params(),
    )(cross, other)

    mine = lax.dynamic_slice_in_dim(solved, col_index * width, width, 2)
    far = (col_index + group) % col_count
    sent = lax.dynamic_slice_in_dim(solved, far * width, width, 2)
    arrived = lax.ppermute(sent, "col", ring(col_count, group))
    interpolation = jnp.where(box == 0, jnp.stack([mine, arrived]), jnp.stack([arrived, mine]))

    buffer = pl.pallas_call(
        functools.partial(update_kernel, box_count, box_total, entries),
        out_shape=jax.ShapeDtypeStruct((3 * box_count, 2, S, S), jnp.float32),
        in_specs=[SMEM, SMEM, VMEM, VMEM, VMEM],
        out_specs=VMEM,
        compiler_params=params(),
    )(where, neighbour_boxes, kern, solved, pivots)

    strip = S // col_count
    block = (box_count, 2, strip, S)
    skeleton_update = pl.pallas_call(
        functools.partial(reduce_kernel, box_total, col_count, group),
        out_shape=jax.ShapeDtypeStruct(block, jnp.float32),
        in_specs=[VMEM],
        out_specs=VMEM,
        scratch_shapes=[
            pltpu.VMEM((3, 2) + block, jnp.float32),
            pltpu.VMEM((3,) + block, jnp.float32),
            pltpu.VMEM((3,) + block, jnp.float32),
            pltpu.VMEM((3,) + block, jnp.float32),
            pltpu.VMEM((2,) + block, jnp.float32),
            pltpu.SemaphoreType.DMA((11,)),
            pltpu.SemaphoreType.DMA((11,)),
        ],
        compiler_params=params(collective_id=1, has_side_effects=True),
    )(buffer.reshape(3 * box_count, 2, col_count, strip, S))
    return (interpolation, skeleton_update)


def solution(mesh):
    placed = (
        P("box", None, None),
        P(None, "col"),
        P("box", None),
        P("box", None),
        P("box", None),
        P("box", None, "col"),
    )
    return jax.shard_map(
        on_device,
        mesh=mesh,
        in_specs=placed,
        out_specs=(P("box", None, None, "col"), P("box", None, "col", None)),
        check_vma=False,
    )
```

```python
import functools
import math

import jax
import jax.numpy as jnp
from jax import lax
from jax.experimental import pallas as pl
from jax.experimental.pallas import tpu as pltpu
from jax.sharding import PartitionSpec as P

S = 256

softening = 0.05
proxy_radius = 1.5
ridge_share = 0.05
highest = lax.Precision.HIGHEST
NBLK = 32
ROWS = 16

COS = (1.4142135381698608, -6.978850841522217, 5.739460468292236, -1.883557915687561, 0.3106880187988281)
SIN = (4.442883014678955, -7.308245658874512, 3.606354236602783, -0.8461116552352905, 0.1098245158791542)

VMEM = pl.BlockSpec(memory_space=pltpu.VMEM)
SMEM = pl.BlockSpec(memory_space=pltpu.SMEM)


def params(**more):
    return pltpu.CompilerParams(vmem_limit_bytes=48 * 1024 * 1024, **more)


def horner(coefficients, z):
    total = jnp.full_like(z, coefficients[-1])
    for one in coefficients[-2::-1]:
        total = total * z + one
    return total


def kernel_values(tx, ty, tz, sx, sy, sz):
    dx = tx - sx
    dy = ty - sy
    dz = tz - sz
    square = (dx * dx + dy * dy) + (dz * dz + 4.0 * softening * softening)
    inverse = lax.rsqrt(square)
    turns = square * inverse
    part = turns - jnp.floor(turns + 0.5)
    z = part * part
    amplitude = inverse * (1.0 / (2.0 * math.pi))
    sine = part * horner(SIN, z)
    scaled = amplitude * sine
    return amplitude - scaled * sine, scaled * horner(COS, z)


def slot_of(nb_ref, where_ref, row, entry, box_count, box_total):
    owner_box = nb_ref[row, entry]
    step = owner_box // box_count - where_ref[0] + 1
    step = jnp.where(step < 0, step + box_total, step)
    step = jnp.where(step >= box_total, step - box_total, step)
    return step * box_count + owner_box % box_count


def dot_tn(a, b):
    return lax.dot_general(a, b, (((0,), (0,)), ((), ())), preferred_element_type=jnp.float32)


def tile_kernel(box_count, box_total, entries, where_ref, nb_ref, place_ref, points_ref, order_ref,
                proxy_ref, cross_ref, kern_ref, tcol, srow, raw, tiles, total):
    count = points_ref.shape[3]
    share = proxy_ref.shape[2]
    proxies = box_count * share
    raw[...] = jnp.zeros_like(raw)
    box = where_ref[1]
    first = where_ref[2] * entries

    def ordered(slot):
        side, which = slot // box_count, slot % box_count
        one_hot = (
            lax.broadcasted_iota(jnp.int32, (count, count), 0)
            == order_ref[side, pl.ds(which, 1), :]
        ).astype(jnp.float32).astype(jnp.bfloat16)
        raw[0:3, :] = points_ref[side, which]
        whole = raw[...]
        top = whole.astype(jnp.bfloat16).astype(jnp.float32)
        mid = (whole - top).astype(jnp.bfloat16).astype(jnp.float32)
        rows = jnp.concatenate([top, mid, whole - top - mid, jnp.zeros_like(top)], axis=0)
        picked = jnp.dot(rows.astype(jnp.bfloat16), one_hot, preferred_element_type=jnp.float32)
        return (picked[0:8] + picked[8:16]) + picked[16:24]

    axis_row = lax.broadcasted_iota(jnp.int32, (8, count), 0)
    srow[...] = 2.0 * ordered(box_count + box)
    for k in range(entries):
        slot = slot_of(nb_ref, where_ref, box, first + k, box_count, box_total)
        code = place_ref[box, first + k]
        code = jnp.where(code >= 13, code + 1, code)
        shift = [(code // 9 - 1), (code // 3) % 3 - 1, code % 3 - 1]
        move = jnp.where(
            axis_row == 0,
            shift[0].astype(jnp.float32),
            jnp.where(axis_row == 1, shift[1].astype(jnp.float32), shift[2].astype(jnp.float32)),
        )
        start = proxies + k * count
        tcol[start:start + count, 0:8] = jnp.transpose(2.0 * (ordered(slot) + move))
    for d in range(box_count):
        raw[0:3, 0:share] = 2.0 * (0.5 + proxy_radius * proxy_ref[d])
        tcol[d * share:(d + 1) * share, 0:8] = jnp.transpose(raw[:, 0:share])
    block = tiles.shape[1] // 2

    def evaluate(base, slot, keep=None):
        for i in range(block // ROWS):
            inner = slice(i * ROWS, (i + 1) * ROWS)
            lower = slice(block + i * ROWS, block + (i + 1) * ROWS)
            start = pl.multiple_of(base + i * ROWS, ROWS)
            tx = tcol[pl.ds(start, ROWS), 0:1]
            ty = tcol[pl.ds(start, ROWS), 1:2]
            tz = tcol[pl.ds(start, ROWS), 2:3]
            for c in range(0, count, 256):
                here = slice(c, c + 256)
                there = slice(count + c, count + c + 256)
                real, imag = kernel_values(tx, ty, tz, srow[0:1, here], srow[1:2, here],
                                           srow[2:3, here])
                if keep is not None:
                    kern_ref[keep, 0, inner, here] = real
                    kern_ref[keep, 1, inner, here] = imag
                real = real.astype(jnp.bfloat16)
                imag = imag.astype(jnp.bfloat16)
                tiles[slot, inner, here] = real
                tiles[slot, inner, there] = imag
                tiles[slot, lower, here] = imag
                tiles[slot, lower, there] = -real

    def gather(slot):
        total[...] += dot_tn(tiles[slot, :, 0:S], tiles[slot])

    total[...] = jnp.zeros_like(total)
    evaluate(0, 0)
    for i in range(1, proxies // block):
        gather((i + 1) % 2)
        evaluate(i * block, i % 2)
    parity = (proxies // block) % 2
    per = count // block

    @pl.loop(0, entries)
    def _(k):
        base = proxies + k * count
        for i in range(per):
            gather((parity + i + 1) % 2)
            evaluate(base + i * block, (parity + i) % 2, k if i == 0 else None)

    gather((parity + per - 1) % 2)
    cross_ref[0] = total[:, 0:count]
    cross_ref[1] = total[:, count:]


def exact(a, b, dims=((1,), (0,))):
    return lax.dot_general(a, b, (dims, ((), ())), precision=highest,
                           preferred_element_type=jnp.float32)


def solve_kernel(mine_ref, other_ref, x_ref, mat, low, high):
    n = x_ref.shape[1]
    wide = mine_ref.shape[2]
    nb = NBLK
    mat[...] = mine_ref[...] + other_ref[...]
    diagonal = lax.broadcasted_iota(jnp.int32, (n, n), 0) == lax.broadcasted_iota(
        jnp.int32, (n, n), 1
    )
    gram = mat[0, :, 0:n]
    ridge = ridge_share * jnp.sum(jnp.where(diagonal, gram, 0.0)) / n
    mat[0, :, 0:n] = gram + jnp.where(diagonal, ridge, 0.0)
    low[...] = jnp.zeros_like(low)
    high[...] = jnp.zeros_like(high)
    lane = lax.broadcasted_iota(jnp.int32, (nb, 128), 1)
    sub = lax.broadcasted_iota(jnp.int32, (nb, 128), 0)
    lane_all = lax.broadcasted_iota(jnp.int32, (n, 128), 1)

    def turned(block, shift):
        return pltpu.roll(block, shift, 1) if shift else block

    def inverse(block_re, block_im, back):
        re0, im0 = turned(block_re, back), turned(block_im, back)
        re1, im1 = turned(block_re, (back + nb) % 128), turned(block_im, (back + nb) % 128)
        zero = jnp.zeros_like(re0)
        m = jnp.where(lane < nb, re0, jnp.where(lane < 2 * nb, im1,
                                                jnp.where(lane - 2 * nb == sub, 1.0, zero)))
        w = jnp.where(lane < nb, -im0, jnp.where(lane < 2 * nb, re1,
                                                 jnp.where(lane - 3 * nb == sub, 1.0, zero)))

        def spread(block, k):
            return jnp.broadcast_to(block[:, k:k + 1], (nb, 128))

        for k in range(0, nb, 2):
            p0, p1 = spread(m, k), spread(m, k + 1)
            s0, s1 = spread(m, nb + k), spread(m, nb + k + 1)
            a, d = p0[k:k + 1], p1[k + 1:k + 2]
            br, bi = p1[k:k + 1], s1[k:k + 1]
            scale = 1.0 / (a * d - (br * br + bi * bi))
            m0, m1, w0, w1 = m[k:k + 1], m[k + 1:k + 2], w[k:k + 1], w[k + 1:k + 2]
            row_m0 = (d * m0 - (br * m1 + bi * w1)) * scale
            row_w0 = (d * w0 - (br * w1 - bi * m1)) * scale
            row_m1 = (a * m1 - (br * m0 - bi * w0)) * scale
            row_w1 = (a * w1 - (br * w0 + bi * m0)) * scale
            new_m = m - ((p0 * row_m0 + s0 * row_w0) + (p1 * row_m1 + s1 * row_w1))
            new_w = w - ((p0 * row_w0 - s0 * row_m0) + (p1 * row_w1 - s1 * row_m1))
            m = jnp.where(sub == k, row_m0, jnp.where(sub == k + 1, row_m1, new_m))
            w = jnp.where(sub == k, row_w0, jnp.where(sub == k + 1, row_w1, new_w))
        return m

    m = inverse(mat[0, 0:nb, 0:128], mat[1, 0:nb, 0:128], 0)
    for j in range(n // nb):
        rows = slice(j * nb, (j + 1) * nb)
        after = slice((j + 1) * nb, (j + 2) * nb)
        q = (j * nb) // 128 * 128
        back = (128 - (j * nb) % 128) % 128
        start = (j + 1) * nb // 128 * 128
        span = wide - start
        panel_re = mat[0, rows, start:]
        panel_im = mat[1, rows, start:]
        high[2 * nb:3 * nb, 0:span] = panel_re
        high[2 * nb:3 * nb, span:2 * span] = panel_im
        high[3 * nb:4 * nb, 0:span] = -panel_im
        high[3 * nb:4 * nb, span:2 * span] = panel_re
        solved = exact(m, high[:, 0:2 * span])
        low[0:nb, 0:2 * span] = solved
        low[nb:2 * nb, 0:span] = -solved[:, span:]
        low[nb:2 * nb, span:2 * span] = solved[:, 0:span]
        left = jnp.where(
            lane_all < nb,
            turned(mat[0, :, q:q + 128], back),
            jnp.where(lane_all < 2 * nb, turned(mat[1, :, q:q + 128], (back + nb) % 128), 0.0),
        )
        if (j + 1) * nb < n:
            ahead = left[after]
            next_re = mat[0, after, start:start + 128] - exact(ahead, low[:, 0:128])
            next_im = mat[1, after, start:start + 128] - exact(ahead, low[:, span:span + 128])
            m = inverse(next_re, next_im, (128 - ((j + 1) * nb) % 128) % 128)
        change = exact(left, low[:, 0:2 * span])
        mat[0, :, start:] = mat[0, :, start:] - change[:, 0:span]
        mat[1, :, start:] = mat[1, :, start:] - change[:, span:]
        mat[0, rows, start:] = solved[:, 0:span]
        mat[1, rows, start:] = solved[:, span:]
    x_ref[...] = mat[:, :, n:]


def split(x):
    high = x.astype(jnp.bfloat16)
    return high, (x - high.astype(jnp.float32)).astype(jnp.bfloat16)


def threefold(a, b, dims=((1,), (0,))):
    def one(x, y):
        return lax.dot_general(x, y, (dims, ((), ())), preferred_element_type=jnp.float32)

    return one(a[0], b[0]) + (one(a[0], b[1]) + one(a[1], b[0]))


def update_kernel(box_count, box_total, entries, where_ref, nb_ref, kern_ref, x_ref, pivot_ref,
                  out_ref):
    n = x_ref.shape[1]
    box = where_ref[1]
    first = where_ref[2] * entries
    out_ref[...] = jnp.zeros_like(out_ref)
    xr, xi = x_ref[0], x_ref[1]
    right = split(jnp.concatenate(
        [jnp.concatenate([xr, xi], axis=1), jnp.concatenate([-xi, xr], axis=1)], axis=0))
    pieces = range(pivot_ref.shape[0])
    qr = jnp.concatenate([pivot_ref[c, box, 0:1, :] for c in pieces], axis=1)
    qi = jnp.concatenate([pivot_ref[c, box, 1:2, :] for c in pieces], axis=1)
    nt = ((1,), (1,))
    for k in range(entries):
        slot = slot_of(nb_ref, where_ref, box, first + k, box_count, box_total)
        left = split(jnp.concatenate([kern_ref[k, 0, :, 0:n], kern_ref[k, 1, :, 0:n]], axis=1))
        both = threefold(left, right)
        br = kern_ref[k, 0, :, n:] - both[:, 0:n]
        bi = kern_ref[k, 1, :, n:] - both[:, n:]
        wr = split(br * qr - bi * qi)
        wi = split(br * qi + bi * qr)
        sr, si = split(br), split(bi)
        out_ref[slot, 0] = out_ref[slot, 0] - (threefold(wr, sr, nt) - threefold(wi, si, nt))
        out_ref[slot, 1] = out_ref[slot, 1] - (threefold(wr, si, nt) + threefold(wi, sr, nt))


MESH = pl.DeviceIdType.MESH


def meet(peers):
    barrier = pltpu.get_barrier_semaphore()
    for peer in peers:
        pl.semaphore_signal(barrier, inc=1, device_id=peer, device_id_type=MESH)
    pl.semaphore_wait(barrier, len(peers))


def exchange_kernel(box_total, col_count, group, points_ref, order_ref, proxy_ref, pivot_ref,
                    points_out, order_out, proxy_out, pivot_out, send, recv, local):
    me = lax.axis_index("col")
    place = lax.axis_index("box")
    after = {"box": lax.rem(place + 1, box_total)}
    before = {"box": lax.rem(place + box_total - 1, box_total)}
    peers = [{"col": lax.rem(me + d, col_count)} for d in range(1, col_count)]
    meet([before, after] + peers)
    jobs = [
        (points_ref, points_out.at[0], after),
        (points_ref, points_out.at[2], before),
        (order_ref, order_out.at[0], after),
        (order_ref, order_out.at[2], before),
    ]
    for d in range(1, col_count):
        jobs.append((pivot_ref, pivot_out.at[me], peers[d - 1]))
        if d % group == 0:
            jobs.append((proxy_ref, proxy_out.at[d // group], peers[d - 1]))
    copies = []
    for i, (source, target, peer) in enumerate(jobs):
        copy = pltpu.make_async_remote_copy(
            src_ref=source, dst_ref=target, send_sem=send.at[i], recv_sem=recv.at[i],
            device_id=peer, device_id_type=MESH)
        copy.start()
        copies.append(copy)
    own = ((points_ref, points_out.at[1]), (order_ref, order_out.at[1]),
           (proxy_ref, proxy_out.at[0]), (pivot_ref, pivot_out.at[me]))
    for i, (source, target) in enumerate(own):
        copy = pltpu.make_async_copy(source, target, local.at[i])
        copy.start()
        copies.append(copy)
    for copy in copies:
        copy.wait()


def swap_kernel(mine_ref, other_ref, send, recv):
    me = lax.axis_index("col")
    peer = {"col": me + 1 - 2 * lax.rem(me, 2)}
    meet([peer])
    copies = []
    for i in range(mine_ref.shape[0]):
        copy = pltpu.make_async_remote_copy(
            src_ref=mine_ref.at[i], dst_ref=other_ref.at[i], send_sem=send.at[i],
            recv_sem=recv.at[i], device_id=peer, device_id_type=MESH)
        copy.start()
        copies.append(copy)
    for copy in copies:
        copy.wait()


def reduce_kernel(box_total, col_count, group, buf_ref, out_ref, pair_in, cross_out, cross_in,
                  held, box_in, send, recv):
    me = lax.axis_index("col")
    place = lax.axis_index("box")
    partner = me + 1 - 2 * lax.rem(me, 2)
    across = lax.rem(me + group, col_count)
    far = lax.rem(partner + group, col_count)
    near_id, far_id = {"col": partner}, {"col": across}
    after = {"box": lax.rem(place + 1, box_total)}
    before = {"box": lax.rem(place + box_total - 1, box_total)}
    meet([near_id, far_id, before, after])
    width = out_ref.shape[0]

    def copy(index, source, target, peer):
        one = pltpu.make_async_remote_copy(
            src_ref=source, dst_ref=target, send_sem=send.at[index], recv_sem=recv.at[index],
            device_id=peer, device_id_type=MESH)
        one.start()
        return one

    box = me // group
    fed = 1 - box
    pairs = {}
    for kind, block in ((0, far), (1, partner)):
        for g in (0, 2):
            source = buf_ref.at[pl.ds(g * width, width), :, block]
            pairs[g, kind] = copy(2 * g + kind, source, pair_in.at[g, kind], near_id)
        pairs[1, kind] = copy(2 + kind, buf_ref.at[width + fed, :, block],
                              pair_in.at[1, kind, 0], near_id)
    cross = {}
    for g in (0, 2):
        pairs[g, 0].wait()
        cross_out[g] = buf_ref[g * width:(g + 1) * width, :, across] + pair_in[g, 0]
        cross[g] = copy(6 + g, cross_out.at[g], cross_in.at[g], far_id)
    pairs[1, 0].wait()
    cross_out[1, 0] = buf_ref[width + fed, :, across] + pair_in[1, 0, 0]
    cross[1] = copy(7, cross_out.at[1, 0], cross_in.at[1, 0], far_id)
    for g in (0, 2):
        pairs[g, 1].wait()
        held[g] = buf_ref[g * width:(g + 1) * width, :, me] + pair_in[g, 1]
    pairs[1, 1].wait()
    held[1, fed] = buf_ref[width + fed, :, me] + pair_in[1, 1, 0]
    moves = []
    for side, (g, peer) in enumerate(((0, before), (2, after))):
        cross[g].wait()
        held[g] = held[g] + cross_in[g]
        moves.append(copy(9 + side, held.at[g], box_in.at[side], peer))
    cross[1].wait()
    held[1, box] = cross_in[1, 0]
    moves[0].wait()
    held[1] = held[1] + box_in[0]
    moves[1].wait()
    out_ref[...] = held[1] + box_in[1]


def ring(count, step):
    return [(i, (i + step) % count) for i in range(count)]


def on_device(
    box_points, proxy_directions, point_order, neighbour_boxes, neighbour_places, pivot_inverse
):
    box_count, _, point_count = box_points.shape
    col_count = lax.axis_size("col")
    box_total = lax.axis_size("box")
    col_index = lax.axis_index("col")
    box_index = lax.axis_index("box")
    group = col_count // box_count
    box = col_index // group
    part = col_index % group
    entries = neighbour_boxes.shape[1] // group
    width = pivot_inverse.shape[2]
    where = jnp.stack([box_index, box, part]).astype(jnp.int32)

    jobs = 4 + col_count - 1 + box_count - 1
    points, order, proxies, pivots = pl.pallas_call(
        functools.partial(exchange_kernel, box_total, col_count, group),
        out_shape=(
            jax.ShapeDtypeStruct((3,) + box_points.shape, jnp.float32),
            jax.ShapeDtypeStruct((3,) + point_order.shape, jnp.int32),
            jax.ShapeDtypeStruct((box_count,) + proxy_directions.shape, jnp.float32),
            jax.ShapeDtypeStruct((col_count,) + pivot_inverse.shape, jnp.float32),
        ),
        in_specs=[pl.BlockSpec(memory_space=pl.ANY)] * 4,
        out_specs=(VMEM,) * 4,
        scratch_shapes=[pltpu.SemaphoreType.DMA((jobs,)), pltpu.SemaphoreType.DMA((jobs,)),
                        pltpu.SemaphoreType.DMA((4,))],
        compiler_params=pltpu.CompilerParams(collective_id=0, has_side_effects=True),
    )(box_points, point_order, proxy_directions, pivot_inverse)

    share = proxy_directions.shape[1]
    rows = box_count * share + entries * point_count
    cross, kern = pl.pallas_call(
        functools.partial(tile_kernel, box_count, box_total, entries),
        out_shape=(
            jax.ShapeDtypeStruct((2, S, point_count), jnp.float32),
            jax.ShapeDtypeStruct((entries, 2, S, point_count), jnp.float32),
        ),
        in_specs=[SMEM, SMEM, SMEM, VMEM, VMEM, VMEM],
        out_specs=(VMEM, VMEM),
        scratch_shapes=[
            pltpu.VMEM((rows, 128), jnp.float32),
            pltpu.VMEM((8, point_count), jnp.float32),
            pltpu.VMEM((8, point_count), jnp.float32),
            pltpu.VMEM((2, 2 * S, 2 * point_count), jnp.bfloat16),
            pltpu.VMEM((S, 2 * point_count), jnp.float32),
        ],
        compiler_params=params(),
    )(where, neighbour_boxes, neighbour_places, points, order, proxies)

    other = pl.pallas_call(
        swap_kernel,
        out_shape=jax.ShapeDtypeStruct(cross.shape, jnp.float32),
        in_specs=[VMEM],
        out_specs=VMEM,
        scratch_shapes=[pltpu.SemaphoreType.DMA((2,)), pltpu.SemaphoreType.DMA((2,))],
        compiler_params=params(collective_id=2, has_side_effects=True),
    )(cross)
    rest = point_count - S
    solved = pl.pallas_call(
        solve_kernel,
        out_shape=jax.ShapeDtypeStruct((2, S, rest), jnp.float32),
        in_specs=[VMEM, VMEM],
        out_specs=VMEM,
        scratch_shapes=[
            pltpu.VMEM((2, S, point_count), jnp.float32),
            pltpu.VMEM((128, 2 * point_count), jnp.float32),
            pltpu.VMEM((128, 2 * point_count), jnp.float32),
        ],
        compiler_params=params(),
    )(cross, other)

    mine = lax.dynamic_slice_in_dim(solved, col_index * width, width, 2)
    far = (col_index + group) % col_count
    sent = lax.dynamic_slice_in_dim(solved, far * width, width, 2)
    arrived = lax.ppermute(sent, "col", ring(col_count, group))
    interpolation = jnp.where(box == 0, jnp.stack([mine, arrived]), jnp.stack([arrived, mine]))

    buffer = pl.pallas_call(
        functools.partial(update_kernel, box_count, box_total, entries),
        out_shape=jax.ShapeDtypeStruct((3 * box_count, 2, S, S), jnp.float32),
        in_specs=[SMEM, SMEM, VMEM, VMEM, VMEM],
        out_specs=VMEM,
        compiler_params=params(),
    )(where, neighbour_boxes, kern, solved, pivots)

    strip = S // col_count
    block = (box_count, 2, strip, S)
    skeleton_update = pl.pallas_call(
        functools.partial(reduce_kernel, box_total, col_count, group),
        out_shape=jax.ShapeDtypeStruct(block, jnp.float32),
        in_specs=[VMEM],
        out_specs=VMEM,
        scratch_shapes=[
            pltpu.VMEM((3, 2) + block, jnp.float32),
            pltpu.VMEM((3,) + block, jnp.float32),
            pltpu.VMEM((3,) + block, jnp.float32),
            pltpu.VMEM((3,) + block, jnp.float32),
            pltpu.VMEM((2,) + block, jnp.float32),
            pltpu.SemaphoreType.DMA((11,)),
            pltpu.SemaphoreType.DMA((11,)),
        ],
        compiler_params=params(collective_id=1, has_side_effects=True),
    )(buffer.reshape(3 * box_count, 2, col_count, strip, S))
    return (interpolation, skeleton_update)


def solution(mesh):
    placed = (
        P("box", None, None),
        P(None, "col"),
        P("box", None),
        P("box", None),
        P("box", None),
        P("box", None, "col"),
    )
    return jax.shard_map(
        on_device,
        mesh=mesh,
        in_specs=placed,
        out_specs=(P("box", None, None, "col"), P("box", None, "col", None)),
        check_vma=False,
    )
```

```python
import functools
import math

import jax
import jax.numpy as jnp
from jax import lax
from jax.experimental import pallas as pl
from jax.experimental.pallas import tpu as pltpu
from jax.sharding import PartitionSpec as P

S = 256

softening = 0.05
proxy_radius = 1.5
ridge_share = 0.05
highest = lax.Precision.HIGHEST
NBLK = 32
ROWS = 16

COS = (1.4142135381698608, -6.978850841522217, 5.739460468292236, -1.883557915687561, 0.3106880187988281)
SIN = (4.442883014678955, -7.308245658874512, 3.606354236602783, -0.8461116552352905, 0.1098245158791542)

VMEM = pl.BlockSpec(memory_space=pltpu.VMEM)
SMEM = pl.BlockSpec(memory_space=pltpu.SMEM)


def params(**more):
    return pltpu.CompilerParams(vmem_limit_bytes=24 * 1024 * 1024, **more)


def horner(coefficients, z):
    total = jnp.full_like(z, coefficients[-1])
    for one in coefficients[-2::-1]:
        total = total * z + one
    return total


def kernel_values(tx, ty, tz, sx, sy, sz):
    dx = tx - sx
    dy = ty - sy
    dz = tz - sz
    square = (dx * dx + dy * dy) + (dz * dz + 4.0 * softening * softening)
    inverse = lax.rsqrt(square)
    turns = square * inverse
    part = turns - jnp.floor(turns + 0.5)
    z = part * part
    amplitude = inverse * (1.0 / (2.0 * math.pi))
    sine = part * horner(SIN, z)
    scaled = amplitude * sine
    return amplitude - scaled * sine, scaled * horner(COS, z)


def slot_of(nb_ref, where_ref, row, entry, box_count, box_total):
    owner_box = nb_ref[row, entry]
    step = owner_box // box_count - where_ref[0] + 1
    step = jnp.where(step < 0, step + box_total, step)
    step = jnp.where(step >= box_total, step - box_total, step)
    return step * box_count + owner_box % box_count


def dot_tn(a, b):
    return lax.dot_general(a, b, (((0,), (0,)), ((), ())), preferred_element_type=jnp.float32)


def tile_kernel(box_count, box_total, entries, where_ref, nb_ref, place_ref, points_ref, order_ref,
                proxy_ref, cross_ref, kern_ref, tcol, srow, raw, tiles, total):
    count = points_ref.shape[3]
    share = proxy_ref.shape[2]
    proxies = box_count * share
    raw[...] = jnp.zeros_like(raw)
    box = where_ref[1]
    first = where_ref[2] * entries

    def ordered(slot):
        side, which = slot // box_count, slot % box_count
        one_hot = (
            lax.broadcasted_iota(jnp.int32, (count, count), 0)
            == order_ref[side, pl.ds(which, 1), :]
        ).astype(jnp.float32).astype(jnp.bfloat16)
        raw[0:3, :] = points_ref[side, which]
        whole = raw[...]
        top = whole.astype(jnp.bfloat16).astype(jnp.float32)
        mid = (whole - top).astype(jnp.bfloat16).astype(jnp.float32)
        rows = jnp.concatenate([top, mid, whole - top - mid, jnp.zeros_like(top)], axis=0)
        picked = jnp.dot(rows.astype(jnp.bfloat16), one_hot, preferred_element_type=jnp.float32)
        return (picked[0:8] + picked[8:16]) + picked[16:24]

    axis_row = lax.broadcasted_iota(jnp.int32, (8, count), 0)
    srow[...] = 2.0 * ordered(box_count + box)
    for k in range(entries):
        slot = slot_of(nb_ref, where_ref, box, first + k, box_count, box_total)
        code = place_ref[box, first + k]
        code = jnp.where(code >= 13, code + 1, code)
        shift = [(code // 9 - 1), (code // 3) % 3 - 1, code % 3 - 1]
        move = jnp.where(
            axis_row == 0,
            shift[0].astype(jnp.float32),
            jnp.where(axis_row == 1, shift[1].astype(jnp.float32), shift[2].astype(jnp.float32)),
        )
        start = proxies + k * count
        tcol[start:start + count, 0:8] = jnp.transpose(2.0 * (ordered(slot) + move))
    for d in range(box_count):
        raw[0:3, 0:share] = 2.0 * (0.5 + proxy_radius * proxy_ref[d])
        tcol[d * share:(d + 1) * share, 0:8] = jnp.transpose(raw[:, 0:share])
    block = tiles.shape[1] // 2

    def evaluate(base, slot, keep=None):
        for i in range(block // ROWS):
            inner = slice(i * ROWS, (i + 1) * ROWS)
            lower = slice(block + i * ROWS, block + (i + 1) * ROWS)
            start = pl.multiple_of(base + i * ROWS, ROWS)
            tx = tcol[pl.ds(start, ROWS), 0:1]
            ty = tcol[pl.ds(start, ROWS), 1:2]
            tz = tcol[pl.ds(start, ROWS), 2:3]
            for c in range(0, count, 256):
                here = slice(c, c + 256)
                there = slice(count + c, count + c + 256)
                real, imag = kernel_values(tx, ty, tz, srow[0:1, here], srow[1:2, here],
                                           srow[2:3, here])
                if keep is not None:
                    kern_ref[keep, 0, inner, here] = real
                    kern_ref[keep, 1, inner, here] = imag
                real = real.astype(jnp.bfloat16)
                imag = imag.astype(jnp.bfloat16)
                tiles[slot, inner, here] = real
                tiles[slot, inner, there] = imag
                tiles[slot, lower, here] = imag
                tiles[slot, lower, there] = -real

    def gather(slot):
        total[...] += dot_tn(tiles[slot, :, 0:S], tiles[slot])

    total[...] = jnp.zeros_like(total)
    evaluate(0, 0)
    for i in range(1, proxies // block):
        gather((i + 1) % 2)
        evaluate(i * block, i % 2)
    parity = (proxies // block) % 2
    per = count // block

    @pl.loop(0, entries)
    def _(k):
        base = proxies + k * count
        for i in range(per):
            gather((parity + i + 1) % 2)
            evaluate(base + i * block, (parity + i) % 2, k if i == 0 else None)

    gather((parity + per - 1) % 2)
    cross_ref[0] = total[:, 0:count]
    cross_ref[1] = total[:, count:]


def exact(a, b, dims=((1,), (0,))):
    return lax.dot_general(a, b, (dims, ((), ())), precision=highest,
                           preferred_element_type=jnp.float32)


def solve_kernel(mine_ref, other_ref, x_ref, mat, low, high):
    n = x_ref.shape[1]
    wide = mine_ref.shape[2]
    nb = NBLK
    mat[...] = mine_ref[...] + other_ref[...]
    diagonal = lax.broadcasted_iota(jnp.int32, (n, n), 0) == lax.broadcasted_iota(
        jnp.int32, (n, n), 1
    )
    gram = mat[0, :, 0:n]
    ridge = ridge_share * jnp.sum(jnp.where(diagonal, gram, 0.0)) / n
    mat[0, :, 0:n] = gram + jnp.where(diagonal, ridge, 0.0)
    low[...] = jnp.zeros_like(low)
    high[...] = jnp.zeros_like(high)
    lane = lax.broadcasted_iota(jnp.int32, (nb, 128), 1)
    sub = lax.broadcasted_iota(jnp.int32, (nb, 128), 0)
    lane_all = lax.broadcasted_iota(jnp.int32, (n, 128), 1)

    def turned(block, shift):
        return pltpu.roll(block, shift, 1) if shift else block

    def inverse(block_re, block_im, back):
        re0, im0 = turned(block_re, back), turned(block_im, back)
        re1, im1 = turned(block_re, (back + nb) % 128), turned(block_im, (back + nb) % 128)
        zero = jnp.zeros_like(re0)
        m = jnp.where(lane < nb, re0, jnp.where(lane < 2 * nb, im1,
                                                jnp.where(lane - 2 * nb == sub, 1.0, zero)))
        w = jnp.where(lane < nb, -im0, jnp.where(lane < 2 * nb, re1,
                                                 jnp.where(lane - 3 * nb == sub, 1.0, zero)))

        def spread(block, k):
            return jnp.broadcast_to(block[:, k:k + 1], (nb, 128))

        for k in range(0, nb, 2):
            p0, p1 = spread(m, k), spread(m, k + 1)
            s0, s1 = spread(m, nb + k), spread(m, nb + k + 1)
            a, d = p0[k:k + 1], p1[k + 1:k + 2]
            br, bi = p1[k:k + 1], s1[k:k + 1]
            scale = 1.0 / (a * d - (br * br + bi * bi))
            m0, m1, w0, w1 = m[k:k + 1], m[k + 1:k + 2], w[k:k + 1], w[k + 1:k + 2]
            row_m0 = (d * m0 - (br * m1 + bi * w1)) * scale
            row_w0 = (d * w0 - (br * w1 - bi * m1)) * scale
            row_m1 = (a * m1 - (br * m0 - bi * w0)) * scale
            row_w1 = (a * w1 - (br * w0 + bi * m0)) * scale
            new_m = m - ((p0 * row_m0 + s0 * row_w0) + (p1 * row_m1 + s1 * row_w1))
            new_w = w - ((p0 * row_w0 - s0 * row_m0) + (p1 * row_w1 - s1 * row_m1))
            m = jnp.where(sub == k, row_m0, jnp.where(sub == k + 1, row_m1, new_m))
            w = jnp.where(sub == k, row_w0, jnp.where(sub == k + 1, row_w1, new_w))
        return m

    m = inverse(mat[0, 0:nb, 0:128], mat[1, 0:nb, 0:128], 0)
    for j in range(n // nb):
        rows = slice(j * nb, (j + 1) * nb)
        after = slice((j + 1) * nb, (j + 2) * nb)
        q = (j * nb) // 128 * 128
        back = (128 - (j * nb) % 128) % 128
        start = (j + 1) * nb // 128 * 128
        span = wide - start
        panel_re = mat[0, rows, start:]
        panel_im = mat[1, rows, start:]
        high[2 * nb:3 * nb, 0:span] = panel_re
        high[2 * nb:3 * nb, span:2 * span] = panel_im
        high[3 * nb:4 * nb, 0:span] = -panel_im
        high[3 * nb:4 * nb, span:2 * span] = panel_re
        solved = exact(m, high[:, 0:2 * span])
        low[0:nb, 0:2 * span] = solved
        low[nb:2 * nb, 0:span] = -solved[:, span:]
        low[nb:2 * nb, span:2 * span] = solved[:, 0:span]
        left = jnp.where(
            lane_all < nb,
            turned(mat[0, :, q:q + 128], back),
            jnp.where(lane_all < 2 * nb, turned(mat[1, :, q:q + 128], (back + nb) % 128), 0.0),
        )
        if (j + 1) * nb < n:
            ahead = left[after]
            next_re = mat[0, after, start:start + 128] - exact(ahead, low[:, 0:128])
            next_im = mat[1, after, start:start + 128] - exact(ahead, low[:, span:span + 128])
            m = inverse(next_re, next_im, (128 - ((j + 1) * nb) % 128) % 128)
        change = exact(left, low[:, 0:2 * span])
        mat[0, :, start:] = mat[0, :, start:] - change[:, 0:span]
        mat[1, :, start:] = mat[1, :, start:] - change[:, span:]
        mat[0, rows, start:] = solved[:, 0:span]
        mat[1, rows, start:] = solved[:, span:]
    x_ref[...] = mat[:, :, n:]


def split(x):
    high = x.astype(jnp.bfloat16)
    return high, (x - high.astype(jnp.float32)).astype(jnp.bfloat16)


def threefold(a, b, dims=((1,), (0,))):
    def one(x, y):
        return lax.dot_general(x, y, (dims, ((), ())), preferred_element_type=jnp.float32)

    return one(a[0], b[0]) + (one(a[0], b[1]) + one(a[1], b[0]))


def update_kernel(box_count, box_total, entries, where_ref, nb_ref, kern_ref, x_ref, pivot_ref,
                  out_ref):
    n = x_ref.shape[1]
    box = where_ref[1]
    first = where_ref[2] * entries
    out_ref[...] = jnp.zeros_like(out_ref)
    xr, xi = x_ref[0], x_ref[1]
    right = split(jnp.concatenate(
        [jnp.concatenate([xr, xi], axis=1), jnp.concatenate([-xi, xr], axis=1)], axis=0))
    pieces = range(pivot_ref.shape[0])
    qr = jnp.concatenate([pivot_ref[c, box, 0:1, :] for c in pieces], axis=1)
    qi = jnp.concatenate([pivot_ref[c, box, 1:2, :] for c in pieces], axis=1)
    nt = ((1,), (1,))
    for k in range(entries):
        slot = slot_of(nb_ref, where_ref, box, first + k, box_count, box_total)
        left = split(jnp.concatenate([kern_ref[k, 0, :, 0:n], kern_ref[k, 1, :, 0:n]], axis=1))
        both = threefold(left, right)
        br = kern_ref[k, 0, :, n:] - both[:, 0:n]
        bi = kern_ref[k, 1, :, n:] - both[:, n:]
        wr = split(br * qr - bi * qi)
        wi = split(br * qi + bi * qr)
        sr, si = split(br), split(bi)
        out_ref[slot, 0] = out_ref[slot, 0] - (threefold(wr, sr, nt) - threefold(wi, si, nt))
        out_ref[slot, 1] = out_ref[slot, 1] - (threefold(wr, si, nt) + threefold(wi, sr, nt))


MESH = pl.DeviceIdType.MESH


def meet(peers):
    barrier = pltpu.get_barrier_semaphore()
    for peer in peers:
        pl.semaphore_signal(barrier, inc=1, device_id=peer, device_id_type=MESH)
    pl.semaphore_wait(barrier, len(peers))


def exchange_kernel(box_total, col_count, group, points_ref, order_ref, proxy_ref, pivot_ref,
                    points_out, order_out, proxy_out, pivot_out, send, recv, local):
    me = lax.axis_index("col")
    place = lax.axis_index("box")
    after = {"box": lax.rem(place + 1, box_total)}
    before = {"box": lax.rem(place + box_total - 1, box_total)}
    peers = [{"col": lax.rem(me + d, col_count)} for d in range(1, col_count)]
    meet([before, after] + peers)
    jobs = [
        (points_ref, points_out.at[0], after),
        (points_ref, points_out.at[2], before),
        (order_ref, order_out.at[0], after),
        (order_ref, order_out.at[2], before),
    ]
    for d in range(1, col_count):
        jobs.append((pivot_ref, pivot_out.at[me], peers[d - 1]))
        if d % group == 0:
            jobs.append((proxy_ref, proxy_out.at[d // group], peers[d - 1]))
    copies = []
    for i, (source, target, peer) in enumerate(jobs):
        copy = pltpu.make_async_remote_copy(
            src_ref=source, dst_ref=target, send_sem=send.at[i], recv_sem=recv.at[i],
            device_id=peer, device_id_type=MESH)
        copy.start()
        copies.append(copy)
    own = ((points_ref, points_out.at[1]), (order_ref, order_out.at[1]),
           (proxy_ref, proxy_out.at[0]), (pivot_ref, pivot_out.at[me]))
    for i, (source, target) in enumerate(own):
        copy = pltpu.make_async_copy(source, target, local.at[i])
        copy.start()
        copies.append(copy)
    for copy in copies:
        copy.wait()


def swap_kernel(mine_ref, other_ref, send, recv):
    me = lax.axis_index("col")
    peer = {"col": me + 1 - 2 * lax.rem(me, 2)}
    meet([peer])
    copies = []
    for i in range(mine_ref.shape[0]):
        copy = pltpu.make_async_remote_copy(
            src_ref=mine_ref.at[i], dst_ref=other_ref.at[i], send_sem=send.at[i],
            recv_sem=recv.at[i], device_id=peer, device_id_type=MESH)
        copy.start()
        copies.append(copy)
    for copy in copies:
        copy.wait()


def reduce_kernel(box_total, col_count, group, buf_ref, out_ref, pair_in, cross_out, cross_in,
                  held, box_in, send, recv):
    me = lax.axis_index("col")
    place = lax.axis_index("box")
    partner = me + 1 - 2 * lax.rem(me, 2)
    across = lax.rem(me + group, col_count)
    far = lax.rem(partner + group, col_count)
    near_id, far_id = {"col": partner}, {"col": across}
    after = {"box": lax.rem(place + 1, box_total)}
    before = {"box": lax.rem(place + box_total - 1, box_total)}
    meet([near_id, far_id, before, after])
    width = out_ref.shape[0]

    def copy(index, source, target, peer):
        one = pltpu.make_async_remote_copy(
            src_ref=source, dst_ref=target, send_sem=send.at[index], recv_sem=recv.at[index],
            device_id=peer, device_id_type=MESH)
        one.start()
        return one

    box = me // group
    fed = 1 - box
    pairs = {}
    for kind, block in ((0, far), (1, partner)):
        for g in (0, 2):
            source = buf_ref.at[pl.ds(g * width, width), :, block]
            pairs[g, kind] = copy(2 * g + kind, source, pair_in.at[g, kind], near_id)
        pairs[1, kind] = copy(2 + kind, buf_ref.at[width + fed, :, block],
                              pair_in.at[1, kind, 0], near_id)
    cross = {}
    for g in (0, 2):
        pairs[g, 0].wait()
        cross_out[g] = buf_ref[g * width:(g + 1) * width, :, across] + pair_in[g, 0]
        cross[g] = copy(6 + g, cross_out.at[g], cross_in.at[g], far_id)
    pairs[1, 0].wait()
    cross_out[1, 0] = buf_ref[width + fed, :, across] + pair_in[1, 0, 0]
    cross[1] = copy(7, cross_out.at[1, 0], cross_in.at[1, 0], far_id)
    for g in (0, 2):
        pairs[g, 1].wait()
        held[g] = buf_ref[g * width:(g + 1) * width, :, me] + pair_in[g, 1]
    pairs[1, 1].wait()
    held[1, fed] = buf_ref[width + fed, :, me] + pair_in[1, 1, 0]
    moves = []
    for side, (g, peer) in enumerate(((0, before), (2, after))):
        cross[g].wait()
        held[g] = held[g] + cross_in[g]
        moves.append(copy(9 + side, held.at[g], box_in.at[side], peer))
    cross[1].wait()
    held[1, box] = cross_in[1, 0]
    moves[0].wait()
    held[1] = held[1] + box_in[0]
    moves[1].wait()
    out_ref[...] = held[1] + box_in[1]


def ring(count, step):
    return [(i, (i + step) % count) for i in range(count)]


def on_device(
    box_points, proxy_directions, point_order, neighbour_boxes, neighbour_places, pivot_inverse
):
    box_count, _, point_count = box_points.shape
    col_count = lax.axis_size("col")
    box_total = lax.axis_size("box")
    col_index = lax.axis_index("col")
    box_index = lax.axis_index("box")
    group = col_count // box_count
    box = col_index // group
    part = col_index % group
    entries = neighbour_boxes.shape[1] // group
    width = pivot_inverse.shape[2]
    where = jnp.stack([box_index, box, part]).astype(jnp.int32)

    jobs = 4 + col_count - 1 + box_count - 1
    points, order, proxies, pivots = pl.pallas_call(
        functools.partial(exchange_kernel, box_total, col_count, group),
        out_shape=(
            jax.ShapeDtypeStruct((3,) + box_points.shape, jnp.float32),
            jax.ShapeDtypeStruct((3,) + point_order.shape, jnp.int32),
            jax.ShapeDtypeStruct((box_count,) + proxy_directions.shape, jnp.float32),
            jax.ShapeDtypeStruct((col_count,) + pivot_inverse.shape, jnp.float32),
        ),
        in_specs=[pl.BlockSpec(memory_space=pl.ANY)] * 4,
        out_specs=(VMEM,) * 4,
        scratch_shapes=[pltpu.SemaphoreType.DMA((jobs,)), pltpu.SemaphoreType.DMA((jobs,)),
                        pltpu.SemaphoreType.DMA((4,))],
        compiler_params=params(collective_id=0, has_side_effects=True),
    )(box_points, point_order, proxy_directions, pivot_inverse)

    share = proxy_directions.shape[1]
    rows = box_count * share + entries * point_count
    cross, kern = pl.pallas_call(
        functools.partial(tile_kernel, box_count, box_total, entries),
        out_shape=(
            jax.ShapeDtypeStruct((2, S, point_count), jnp.float32),
            jax.ShapeDtypeStruct((entries, 2, S, point_count), jnp.float32),
        ),
        in_specs=[SMEM, SMEM, SMEM, VMEM, VMEM, VMEM],
        out_specs=(VMEM, VMEM),
        scratch_shapes=[
            pltpu.VMEM((rows, 128), jnp.float32),
            pltpu.VMEM((8, point_count), jnp.float32),
            pltpu.VMEM((8, point_count), jnp.float32),
            pltpu.VMEM((2, 2 * S, 2 * point_count), jnp.bfloat16),
            pltpu.VMEM((S, 2 * point_count), jnp.float32),
        ],
        compiler_params=params(),
    )(where, neighbour_boxes, neighbour_places, points, order, proxies)

    other = pl.pallas_call(
        swap_kernel,
        out_shape=jax.ShapeDtypeStruct(cross.shape, jnp.float32),
        in_specs=[VMEM],
        out_specs=VMEM,
        scratch_shapes=[pltpu.SemaphoreType.DMA((2,)), pltpu.SemaphoreType.DMA((2,))],
        compiler_params=params(collective_id=2, has_side_effects=True),
    )(cross)
    rest = point_count - S
    solved = pl.pallas_call(
        solve_kernel,
        out_shape=jax.ShapeDtypeStruct((2, S, rest), jnp.float32),
        in_specs=[VMEM, VMEM],
        out_specs=VMEM,
        scratch_shapes=[
            pltpu.VMEM((2, S, point_count), jnp.float32),
            pltpu.VMEM((128, 2 * point_count), jnp.float32),
            pltpu.VMEM((128, 2 * point_count), jnp.float32),
        ],
        compiler_params=params(),
    )(cross, other)

    mine = lax.dynamic_slice_in_dim(solved, col_index * width, width, 2)
    far = (col_index + group) % col_count
    sent = lax.dynamic_slice_in_dim(solved, far * width, width, 2)
    arrived = lax.ppermute(sent, "col", ring(col_count, group))
    interpolation = jnp.where(box == 0, jnp.stack([mine, arrived]), jnp.stack([arrived, mine]))

    buffer = pl.pallas_call(
        functools.partial(update_kernel, box_count, box_total, entries),
        out_shape=jax.ShapeDtypeStruct((3 * box_count, 2, S, S), jnp.float32),
        in_specs=[SMEM, SMEM, VMEM, VMEM, VMEM],
        out_specs=VMEM,
        compiler_params=params(),
    )(where, neighbour_boxes, kern, solved, pivots)

    strip = S // col_count
    block = (box_count, 2, strip, S)
    skeleton_update = pl.pallas_call(
        functools.partial(reduce_kernel, box_total, col_count, group),
        out_shape=jax.ShapeDtypeStruct(block, jnp.float32),
        in_specs=[VMEM],
        out_specs=VMEM,
        scratch_shapes=[
            pltpu.VMEM((3, 2) + block, jnp.float32),
            pltpu.VMEM((3,) + block, jnp.float32),
            pltpu.VMEM((3,) + block, jnp.float32),
            pltpu.VMEM((3,) + block, jnp.float32),
            pltpu.VMEM((2,) + block, jnp.float32),
            pltpu.SemaphoreType.DMA((11,)),
            pltpu.SemaphoreType.DMA((11,)),
        ],
        compiler_params=params(collective_id=1, has_side_effects=True),
    )(buffer.reshape(3 * box_count, 2, col_count, strip, S))
    return (interpolation, skeleton_update)


def solution(mesh):
    placed = (
        P("box", None, None),
        P(None, "col"),
        P("box", None),
        P("box", None),
        P("box", None),
        P("box", None, "col"),
    )
    return jax.shard_map(
        on_device,
        mesh=mesh,
        in_specs=placed,
        out_specs=(P("box", None, None, "col"), P("box", None, "col", None)),
        check_vma=False,
    )
```
